256 devices in a mesh: dp: 8 (over x, core), context: 32 (over z, y).
Axes of the slice: x: 4, y: 4, z: 8, core: 2. Of those that a mesh axis runs over, the one named last changes fastest.
Arguments:
- inputs: bfloat16 [8, 16384, 1024], P('dp', 'context'), may hold values from -6 to 6
- step_size: float32 [8, 16384], P('dp', 'context'), may hold values from 0.25 to 16387
- decay_rate: float32 [256], replicated, may hold values from 1.2207031e-05 to 0.125
- frequency: float32 [256], replicated, may hold values from -0.5 to 0.5
- input_proj: bfloat16 [1024, 512], replicated, may hold values from -0.1875 to 0.1875
- output_proj: bfloat16 [1024, 512], replicated, may hold values from -0.25 to 0.25
- skip_gain: float32 [1024], replicated, may hold values from 0.25 to 1.75
- cotangent: bfloat16 [8, 16384, 1024], P('dp', 'context'), may hold values from -6 to 6
Outputs:
- outputs: bfloat16 [8, 16384, 1024], P('dp', 'context')
- input_grad: bfloat16 [8, 16384, 1024], P('dp', 'context')
- input_proj_grad: float32 [1024, 512], P('context')
- output_proj_grad: float32 [1024, 512], P('context')
The draws below stay inside these ranges and needn't reach their ends.
All inputs are finite; a program needn't handle non-finite values.
Results may differ from the reference program's by a relative error of at most 0.0036.
Values sent between devices are 32-bit elements; how exact they have to be, the bound alone decides.
A program may use at most 64 MiB of HBM per device.

```python
import math
import jax
import jax.numpy as jnp
from jax import lax

H = 1024
P_SIZE = 256
L_DEV = 512
SEQS = 8
SEQUENCE_LENGTH = 16384


def draw_step_size(key, part):
    key_base, key_scale, key_first, key_offset = jax.random.split(key, 4)
    block_count = SEQUENCE_LENGTH // L_DEV
    base_steps = jax.random.uniform(key_base, (SEQS, SEQUENCE_LENGTH), jnp.float32, 0.5, 1.5)
    block_scale = jax.random.uniform(key_scale, (SEQS, block_count), jnp.float32, 0.6, 1.4)
    rescaled_values = base_steps * jnp.repeat(block_scale, L_DEV, axis=1)
    leading_position = jax.random.randint(key_first, (SEQS, 1), 0, SEQUENCE_LENGTH)
    offset_spot = jax.random.randint(key_offset, (SEQS, 1), 1, SEQUENCE_LENGTH)
    trailing_position = (leading_position + offset_spot) % SEQUENCE_LENGTH
    token_places = jnp.arange(SEQUENCE_LENGTH, dtype=jnp.int32)[None, :]
    event_marks = (token_places == leading_position).astype(jnp.float32) + (token_places == trailing_position).astype(jnp.float32)
    return rescaled_values + float(SEQUENCE_LENGTH) * event_marks


def draw_decay_rate(key, part):
    key_pick, key_slow, key_fast = jax.random.split(key, 3)
    slow_share = 0.5
    slow_pick = jax.random.uniform(key_pick, (P_SIZE,), jnp.float32) < slow_share
    slow_rates = jnp.exp(jax.random.uniform(key_slow, (P_SIZE,), jnp.float32, math.log(0.2), math.log(0.6))) / float(SEQUENCE_LENGTH)
    fast_rates = jnp.exp(jax.random.uniform(key_fast, (P_SIZE,), jnp.float32, math.log(1.0 / 40.0), math.log(1.0 / 8.0)))
    return jnp.where(slow_pick, slow_rates, fast_rates)


def spiked(drawn, own_key, source, target, parts, factor):
    def block_of(axis_at):
        return (jnp.arange(drawn.shape[axis_at]) // (drawn.shape[axis_at] // parts)).reshape((-1,) + (1,) * (drawn.ndim - 1 - axis_at))

    first = jax.random.permutation(own_key, parts)[block_of(target)]
    other_side = (block_of(target) + parts // 2) % parts
    return jnp.where((block_of(source) == first) | (block_of(source) == other_side), factor * drawn, drawn)


def shard_levels(own_key, dims, cuts, smallest, largest):
    factor_of, own = 1.0, jax.random.fold_in(own_key, 6)
    for axis_at, parts in cuts:
        draws = jnp.exp(jax.random.uniform(jax.random.fold_in(own, axis_at), (parts,), jnp.float32, smallest / len(cuts), largest / len(cuts)))
        factor_of = factor_of * jnp.repeat(draws, dims[axis_at] // parts).reshape([-1 if axis == axis_at else 1 for axis in range(len(dims))])
    return factor_of


def centred(stream_key, extent, deviation, limit, cuts=(), kind=jnp.bfloat16):
    array = jax.random.normal(stream_key, extent, jnp.float32) * deviation
    if len(cuts) > 0:
        array = shard_levels(stream_key, extent, cuts, -0.22, 0.18) * array
    return jnp.clip(array, min=-limit, max=limit).astype(kind)


def heavy_noise(rng, extent, spread, most, shards, heavy, kind=jnp.bfloat16):
    drawn = spread * jax.random.normal(rng, extent, jnp.float32)
    if shards:
        drawn = drawn * shard_levels(rng, extent, shards, -0.22, 0.18)
    return jnp.clip(spiked(drawn, jax.random.fold_in(rng, 3), *heavy), -most, most).astype(kind)


def setup_inputs(seed: int = 0) -> dict:
    key_of = jax.random.split(jax.random.key(seed), 9)
    return {
        "inputs": heavy_noise(key_of[0], (SEQS, SEQUENCE_LENGTH, H), 1.0, 6.0, ((0, 8), (1, 32)), (1, 2, 32, 2.75)),
        "step_size": draw_step_size(jax.random.fold_in(key_of[8], 71), 0),
        "decay_rate": draw_decay_rate(jax.random.fold_in(key_of[8], 71), 0),
        "frequency": jnp.clip(jax.random.uniform(key_of[3], (P_SIZE,), jnp.float32, -0.5, 0.5), -0.5, 0.5),
        "input_proj": centred(key_of[4], (H, 2 * P_SIZE), H ** -0.5, 0.1875),
        "output_proj": centred(key_of[5], (H, 2 * P_SIZE), (2 * P_SIZE) ** -0.5, 0.25),
        "skip_gain": jnp.clip(1.0 + 0.15 * jax.random.normal(key_of[6], (H,), jnp.float32), 0.25, 1.75),
        "cotangent": heavy_noise(key_of[7], (SEQS, SEQUENCE_LENGTH, H), 1.0, 6.0, ((0, 8), (1, 32)), (1, 2, 32, 2.75)),
    }


def sequence_pass(inputs_row, step_row, cotangent_row, decay_rate, frequency, input_proj, output_proj, skip_gain):
    damping = jnp.exp(-step_row[:, None] * decay_rate)
    phase_turn = step_row[:, None] * frequency
    lam_re = damping * jnp.cos(phase_turn)
    lam_im = damping * jnp.sin(phase_turn)
    norm_gain = jnp.sqrt(-jnp.expm1(-2.0 * decay_rate))
    pair_gain = jnp.concatenate([norm_gain, norm_gain])
    state_count = decay_rate.shape[0]
    drive_term = jnp.dot(inputs_row, input_proj, preferred_element_type=jnp.float32) * pair_gain

    def forward_step(carry_pair, slice_pack):
        carry_re, carry_im = carry_pair
        step_re, step_im, push_re, push_im = slice_pack
        new_re = step_re * carry_re - step_im * carry_im + push_re
        new_im = step_re * carry_im + step_im * carry_re + push_im
        return ((new_re, new_im), (new_re, new_im))
    start_pair = (jnp.zeros((state_count,), jnp.float32), jnp.zeros((state_count,), jnp.float32))
    _, (state_re, state_im) = lax.scan(forward_step, start_pair, (lam_re, lam_im, drive_term[:, :state_count], drive_term[:, state_count:]))
    state_pairs = jnp.concatenate([state_re, state_im], axis=1).astype(jnp.bfloat16)
    mixed = jnp.dot(state_pairs, output_proj.T, preferred_element_type=jnp.float32)
    outputs = (mixed + skip_gain * inputs_row.astype(jnp.float32)).astype(jnp.bfloat16)
    adjoint_drive = jnp.dot(cotangent_row, output_proj, preferred_element_type=jnp.float32)
    next_re = jnp.concatenate([lam_re[1:], jnp.zeros_like(lam_re[:1])], axis=0)
    next_im = jnp.concatenate([lam_im[1:], jnp.zeros_like(lam_im[:1])], axis=0)

    def backward_update(carry_pair, slice_pack):
        carry_re, carry_im = carry_pair
        step_re, step_im, push_re, push_im = slice_pack
        new_re = push_re + step_re * carry_re + step_im * carry_im
        new_im = push_im + step_re * carry_im - step_im * carry_re
        return ((new_re, new_im), (new_re, new_im))
    _, (back_re, back_im) = lax.scan(backward_update, start_pair, (next_re, next_im, adjoint_drive[:, :state_count], adjoint_drive[:, state_count:]), reverse=True)
    adjoint_pairs = (jnp.concatenate([back_re, back_im], axis=1) * pair_gain).astype(jnp.bfloat16)
    back_in = jnp.dot(adjoint_pairs, input_proj.T, preferred_element_type=jnp.float32)
    input_grad = (back_in + skip_gain * cotangent_row.astype(jnp.float32)).astype(jnp.bfloat16)
    grad_in_term = jnp.dot(inputs_row.T, adjoint_pairs, preferred_element_type=jnp.float32)
    grad_out_term = jnp.dot(cotangent_row.T, state_pairs, preferred_element_type=jnp.float32)
    return (outputs, input_grad, grad_in_term, grad_out_term)

def reference(inputs, step_size, decay_rate, frequency, input_proj, output_proj, skip_gain, cotangent):

    def one_sequence(seq_pack):
        return sequence_pass(seq_pack[0], seq_pack[1], seq_pack[2], decay_rate, frequency, input_proj, output_proj, skip_gain)
    outputs, input_grad, grad_in_terms, grad_out_terms = lax.map(one_sequence, (inputs, step_size, cotangent))
    grad_scale = float(SEQS * SEQUENCE_LENGTH) ** (-0.5)
    input_proj_grad = lax.optimization_barrier(jnp.sum(grad_in_terms, axis=0)) * grad_scale
    output_proj_grad = lax.optimization_barrier(jnp.sum(grad_out_terms, axis=0)) * grad_scale
    return (outputs, input_grad, input_proj_grad, output_proj_grad)
```

```python
import jax
import jax.numpy as jnp
from jax import lax
from jax.experimental import pallas as pl
from jax.experimental.pallas import tpu as pltpu
from jax.sharding import PartitionSpec as P

MESH = pl.DeviceIdType.MESH
F32, BF16 = jnp.float32, jnp.bfloat16
ROWS, WIDTH, STATES = 512, 1024, 256
SUB = 8
LAPS = ROWS // SUB
NX, NY, NZ = 4, 4, 8
PEERS = NY * NZ
DP = 2 * NX
SCALE = float(8 * 16384) ** -0.5


def turn(time, decay, frequency):
    damping = jnp.exp(-(time * decay))
    phase = time * frequency
    n = jnp.floor(phase * 0.6366197723675814 + 0.5)
    r = ((phase - n * 1.5703125) - n * 4.837512969970703125e-4) - n * 7.54978995489188216e-8
    q = n.astype(jnp.int32)
    z = r * r
    sine = r + r * z * (-1.6666654611e-1 + z * (8.3321608736e-3 + z * -1.9515295891e-4))
    cosine = (1.0 - 0.5 * z) + z * z * (
        4.166664568298827e-2 + z * (-1.388731625493765e-3 + z * 2.443315711809948e-5)
    )
    swap = (q & 1) == 1
    a = jnp.where(swap, sine, cosine)
    b = jnp.where(swap, cosine, sine)
    re = jnp.where(((q + 1) & 2) == 2, -a, a)
    im = jnp.where((q & 2) == 2, -b, b)
    return damping * re, damping * im


def cmul(ar, ai, br, bi):
    return ar * br - ai * bi, ar * bi + ai * br


def cmulc(ar, ai, br, bi):
    return ar * br + ai * bi, ar * bi - ai * br


def kernel(
    x_hbm, step_ref, decay_ref, freq_ref, win_hbm, wout_hbm, skip_ref, cot_hbm,
    out_hbm, ig_hbm, gin_ref, gout_ref,
    xc, wio, xct, stb, lam, drv, pairs, outs, chunk, msg, rmsg, own, theirs, partner,
    r1, r2, r3, fin,
    load_sem, store_sem, pre_sem, pair_sem, ring_sem, z_sem, fin_sem,
):
    dp = lax.axis_index("dp")
    ctx = lax.axis_index("context")
    core, x = lax.rem(dp, 2), lax.div(dp, 2)
    y, z = lax.rem(ctx, NY), lax.div(ctx, NY)
    other = 1 - core

    barrier = pltpu.get_barrier_semaphore()

    def greet_context(d, _):
        pl.semaphore_signal(barrier, inc=1, device_id=(dp, lax.rem(ctx + d, PEERS)), device_id_type=MESH)
        return 0

    def greet_dp(d, _):
        pl.semaphore_signal(barrier, inc=1, device_id=(lax.rem(dp + d, DP), ctx), device_id_type=MESH)
        return 0

    loads = [
        pltpu.make_async_copy(x_hbm, xc.at[0], load_sem.at[0]),
        pltpu.make_async_copy(win_hbm, wio.at[0], load_sem.at[1]),
        pltpu.make_async_copy(cot_hbm, xc.at[1], load_sem.at[2]),
        pltpu.make_async_copy(wout_hbm, wio.at[1], load_sem.at[3]),
    ]
    for load in loads:
        load.start()
    lax.fori_loop(1, PEERS, greet_context, 0)
    lax.fori_loop(1, DP, greet_dp, 0)

    decay = [decay_ref[:, g * 128 : (g + 1) * 128] for g in range(2)]
    freq = [freq_ref[:, g * 128 : (g + 1) * 128] for g in range(2)]
    gain = []
    for g in range(2):
        v = 2.0 * decay[g]
        s = jnp.ones_like(v)
        for k in range(9, 1, -1):
            s = 1.0 - v * (1.0 / k) * s
        gain.append(jnp.sqrt(v * s))

    for r in range(ROWS // 128):
        line = jnp.broadcast_to(step_ref[:, r * 128 : (r + 1) * 128], (128, 128))
        stb[r * 128 : (r + 1) * 128, :] = line.T

    def lam_block(i, _):
        rows = pl.ds(pl.multiple_of(i * 32, 32), 32)
        st = stb[rows, :]
        for g in range(2):
            re, im = turn(st, decay[g], freq[g])
            lam[g, rows, :] = re
            lam[2 + g, rows, :] = im
        return 0

    lax.fori_loop(0, ROWS // 32, lam_block, 0)

    for m in range(2):
        loads[2 * m].wait()
        loads[2 * m + 1].wait()
        for nb in range(2):
            res = jnp.dot(xc[m], wio[m, :, nb * 256 : (nb + 1) * 256], preferred_element_type=F32)
            for g in range(2):
                part = res[:, g * 128 : (g + 1) * 128]
                drv[m, 2 * nb + g] = part * gain[g] if m == 0 else part

    def scan_step(j, carry, store):
        f, b, total = carry[:4], carry[4:8], carry[8]
        rf = pl.ds(j, SUB, stride=LAPS)
        rb = pl.ds(LAPS - 1 - j, SUB, stride=LAPS)
        nf, nb = [None] * 4, [None] * 4
        for g in range(2):
            re, im = cmul(lam[g, rf, :], lam[2 + g, rf, :], f[g], f[2 + g])
            nf[g] = re + drv[0, g, rf, :]
            nf[2 + g] = im + drv[0, 2 + g, rf, :]
            ar = drv[1, g, rb, :] + b[g]
            ai = drv[1, 2 + g, rb, :] + b[2 + g]
            if store:
                drv[0, g, rf, :] = nf[g]
                drv[0, 2 + g, rf, :] = nf[2 + g]
                drv[1, g, rb, :] = ar
                drv[1, 2 + g, rb, :] = ai
            nb[g], nb[2 + g] = cmulc(lam[g, rb, :], lam[2 + g, rb, :], ar, ai)
        if not store:
            total = total + stb[rf, :]
        return (*nf, *nb, total)

    zero = jnp.zeros((SUB, 128), F32)
    summary = lax.fori_loop(0, LAPS, lambda j, c: scan_step(j, c, False), (zero,) * 9)
    for k in range(8):
        chunk[4 + k] = summary[k]
    for g in range(2):
        chunk[g], chunk[2 + g] = turn(jnp.minimum(summary[8], 8.0e6), decay[g], freq[g])
    msg[...] = jnp.zeros_like(msg)

    def pass_chunks(entering, keep):
        f, b = list(entering[:4]), list(entering[4:])
        for s in range(SUB):
            e = SUB - 1 - s
            for g in range(2):
                if keep:
                    for h in (g, 2 + g):
                        chunk[12 + h, s : s + 1, :] = f[h]
                        chunk[16 + h, e : e + 1, :] = b[h]
                re, im = cmul(chunk[g, s : s + 1, :], chunk[2 + g, s : s + 1, :], f[g], f[2 + g])
                f[g] = re + chunk[4 + g, s : s + 1, :]
                f[2 + g] = im + chunk[6 + g, s : s + 1, :]
                re, im = cmulc(chunk[g, e : e + 1, :], chunk[2 + g, e : e + 1, :], b[g], b[2 + g])
                b[g] = re + chunk[8 + g, e : e + 1, :]
                b[2 + g] = im + chunk[10 + g, e : e + 1, :]
        return f + b

    leave = pass_chunks((jnp.zeros((1, 128), F32),) * 8, False)
    total = jnp.sum(summary[8], axis=0, keepdims=True)
    for k in range(4):
        msg[0, k : k + 1, :] = leave[k]
        msg[1, k : k + 1, :] = leave[4 + k]
    msg[0, 4:5, :] = total
    msg[1, 4:5, :] = total
    rmsg[ctx] = jnp.zeros((8, 128), F32)

    pl.semaphore_wait(barrier, PEERS - 1 + DP - 1)

    for dz in (4, 3, 5, 2, 6, 1, 7, 0):
        for dy in (2, 1, 3, 0):
            if dz or dy:
                peer = lax.rem(z + dz, NZ) * NY + lax.rem(y + dy, NY)
                pltpu.make_async_remote_copy(
                    src_ref=msg.at[(peer < ctx).astype(jnp.int32)], dst_ref=rmsg.at[ctx],
                    send_sem=pre_sem.at[0], recv_sem=pre_sem.at[1],
                    device_id=(dp, peer), device_id_type=MESH,
                ).start()

    for m in range(2):
        def turn_block(i, _, m=m):
            cols = pl.ds(pl.multiple_of(i * 128, 128), 128)
            xct[m, cols, :] = xc[m, :, cols].T
            return 0

        lax.fori_loop(0, WIDTH // 128, turn_block, 0)

    everyone = pltpu.make_async_remote_copy(
        src_ref=rmsg.at[pl.ds(0, PEERS - 1)], dst_ref=rmsg.at[pl.ds(0, PEERS - 1)],
        send_sem=pre_sem.at[0], recv_sem=pre_sem.at[1],
        device_id=(dp, lax.rem(ctx + 1, PEERS)), device_id_type=MESH,
    )
    everyone.wait_recv()
    everyone.wait_send()

    place = lax.broadcasted_iota(jnp.int32, (PEERS, 128), 0)
    gap = jnp.zeros((PEERS, 128), F32)
    for i in range(PEERS):
        side = 2 * (i < ctx).astype(jnp.int32) - 1
        gap = gap + jnp.where((i - place) * side > 0, rmsg[i, 4:5, :], 0.0)
    gap = jnp.minimum(gap, 8.0e6)
    sign = jnp.where(place < ctx, 1.0, -1.0)
    entering = [None] * 8
    for g in range(2):
        wr, wi = turn(gap, decay[g], sign * freq[g])
        re, im = cmul(wr, wi, rmsg[:, g, :], rmsg[:, 2 + g, :])
        for h, v in ((g, re), (2 + g, im)):
            entering[h] = jnp.sum(jnp.where(place < ctx, v, 0.0), axis=0, keepdims=True)
            entering[4 + h] = jnp.sum(jnp.where(place > ctx, v, 0.0), axis=0, keepdims=True)
    pass_chunks(entering, True)
    start = tuple(chunk[12 + k] for k in range(8)) + (zero,)
    lax.fori_loop(0, LAPS, lambda j, c: scan_step(j, c, True), start)

    def round_block(i, _):
        rows = pl.ds(pl.multiple_of(i * 32, 32), 32)
        for k in range(4):
            pairs[0, rows, k * 128 : (k + 1) * 128] = (drv[1, k, rows, :] * gain[k % 2]).astype(BF16)
            pairs[1, rows, k * 128 : (k + 1) * 128] = drv[0, k, rows, :].astype(BF16)
        return 0

    lax.fori_loop(0, ROWS // 32, round_block, 0)

    def gradient(m, into):
        def rows_block(i, _):
            rows = pl.ds(pl.multiple_of(i * 256, 256), 256)
            res = jnp.dot(xct[m, rows, :], pairs[m], preferred_element_type=F32)
            for zi in range(2):
                for yy in range(NY):
                    top = (zi * NY + yy) * 32
                    for q in range(NX):
                        a = q + m * (yy - q)
                        b = yy + m * (q - yy)
                        into[a, b, 2 * i + zi] = res[top : top + 32, q * 128 : (q + 1) * 128]
            return 0

        lax.fori_loop(0, WIDTH // 256, rows_block, 0)

    spot = x + core * (y - x)
    spot_other = y + core * (x - y)
    gradient(other, theirs)
    swaps = []
    for k, d in enumerate((2, 1, 3, 0)):
        a = lax.rem(spot_other + d, 4)
        swap = pltpu.make_async_remote_copy(
            src_ref=theirs.at[a], dst_ref=partner.at[k],
            send_sem=pair_sem.at[0, k], recv_sem=pair_sem.at[1, k],
            device_id=(2 * x + other, ctx), device_id_type=MESH,
        )
        swap.start()
        swaps.append(swap)
    gradient(core, own)

    def first_ring(d):
        return (2 * lax.rem(x + other * d, 4) + core, z * NY + lax.rem(y + core * d, 4))

    def second_ring(d):
        return (2 * lax.rem(x + core * d, 4) + core, z * NY + lax.rem(y + other * d, 4))

    def send(src, dst, ring, i, device):
        copy = pltpu.make_async_remote_copy(
            src_ref=src, dst_ref=dst, send_sem=ring_sem.at[ring, 0, i], recv_sem=ring_sem.at[ring, 1, i],
            device_id=device, device_id_type=MESH,
        )
        copy.start()
        return copy

    def take_partner(k, d):
        a = lax.rem(spot + d, 4)
        swaps[k].wait_recv()

        def add(i, _):
            own[a, lax.div(i, 2), pl.ds(lax.rem(i, 2) * 4, 4)] += partner[k, lax.div(i, 2), pl.ds(lax.rem(i, 2) * 4, 4)]
            return 0

        lax.fori_loop(0, 8, add, 0)

    def half1(d, h):
        return own.at[lax.rem(spot + d, 4), pl.ds(2 * h, 2)]

    def half2(d, h):
        return own.at[spot, lax.rem(spot_other + d, 4), pl.ds(4 * h, 4)]

    def add_into(view, buf, blocks):
        def add(i, _):
            if len(view.shape) == 4:
                view[lax.div(i, 8), lax.rem(i, 8)] += buf[lax.div(i, 8), lax.rem(i, 8)]
            else:
                view[i] += buf[i]
            return 0

        lax.fori_loop(0, blocks, add, 0)

    copies = [None] * 6
    take_partner(0, 2)
    copies[0] = send(half1(2, 0), r1.at[0], 0, 0, first_ring(1))
    copies[1] = send(half1(2, 1), r1.at[1], 0, 1, first_ring(3))
    take_partner(1, 1)
    copies[2] = send(half1(1, 1), r1.at[2], 0, 2, first_ring(1))
    take_partner(2, 3)
    copies[3] = send(half1(3, 0), r1.at[3], 0, 3, first_ring(3))
    take_partner(3, 0)

    stores = []
    for m in range(2):
        def out_block(i, _, m=m):
            cols = pl.ds(pl.multiple_of(i * 256, 256), 256)
            mixed = lax.dot_general(
                pairs[1 - m], wio[1 - m, cols, :], (((1,), (1,)), ((), ())), preferred_element_type=F32
            )
            outs[m, :, cols] = (mixed + skip_ref[:, cols] * xc[m, :, cols].astype(F32)).astype(BF16)
            return 0

        lax.fori_loop(0, WIDTH // 256, out_block, 0)
        store = pltpu.make_async_copy(outs.at[m], (out_hbm, ig_hbm)[m], store_sem.at[m])
        store.start()
        stores.append(store)

    copies[0].wait_recv()
    add_into(half1(1, 0), r1.at[0], 16)
    copies[4] = send(half1(1, 0), r1.at[4], 0, 4, first_ring(1))
    copies[1].wait_recv()
    add_into(half1(3, 1), r1.at[1], 16)
    copies[5] = send(half1(3, 1), r1.at[5], 0, 5, first_ring(3))
    copies[3].wait_recv()
    add_into(half1(0, 0), r1.at[3], 16)
    copies[2].wait_recv()
    add_into(half1(0, 1), r1.at[2], 16)
    copies[4].wait_recv()
    add_into(half1(0, 0), r1.at[4], 16)
    copies[5].wait_recv()
    add_into(half1(0, 1), r1.at[5], 16)

    more = [None] * 6
    more[0] = send(half2(2, 0), r2.at[0], 1, 0, second_ring(1))
    more[1] = send(half2(2, 1), r2.at[1], 1, 1, second_ring(3))
    more[2] = send(half2(1, 1), r2.at[2], 1, 2, second_ring(1))
    more[3] = send(half2(3, 0), r2.at[3], 1, 3, second_ring(3))
    more[0].wait_recv()
    add_into(half2(1, 0), r2.at[0], 4)
    more[4] = send(half2(1, 0), r2.at[4], 1, 4, second_ring(1))
    more[1].wait_recv()
    add_into(half2(3, 1), r2.at[1], 4)
    more[5] = send(half2(3, 1), r2.at[5], 1, 5, second_ring(3))
    more[3].wait_recv()
    add_into(half2(0, 0), r2.at[3], 4)
    more[2].wait_recv()
    add_into(half2(0, 1), r2.at[2], 4)
    more[4].wait_recv()
    add_into(half2(0, 0), r2.at[4], 4)
    more[5].wait_recv()
    add_into(half2(0, 1), r2.at[5], 4)

    for dz in (4, 3, 5, 2, 6, 1, 7):
        zz = lax.rem(z + dz, NZ)
        pltpu.make_async_remote_copy(
            src_ref=own.at[spot, spot_other, zz], dst_ref=r3.at[z],
            send_sem=z_sem.at[0], recv_sem=z_sem.at[1],
            device_id=(dp, zz * NY + y), device_id_type=MESH,
        ).start()
    r3[z] = own[spot, spot_other, z]
    column = pltpu.make_async_remote_copy(
        src_ref=r3.at[pl.ds(0, NZ - 1)], dst_ref=r3.at[pl.ds(0, NZ - 1)],
        send_sem=z_sem.at[0], recv_sem=z_sem.at[1],
        device_id=(dp, lax.rem(z + 1, NZ) * NY + y), device_id_type=MESH,
    )
    column.wait_recv()
    column.wait_send()
    piece = r3[0]
    for k in range(1, NZ):
        piece = piece + r3[k]
    mine = core * NX + x
    fin[mine] = piece * SCALE
    for d in (4, 5, 3, 2, 6, 7, 1):
        peer = lax.rem(dp + d, DP)
        pltpu.make_async_remote_copy(
            src_ref=fin.at[mine], dst_ref=fin.at[mine],
            send_sem=fin_sem.at[0], recv_sem=fin_sem.at[1],
            device_id=(peer, ctx), device_id_type=MESH,
        ).start()
    row = pltpu.make_async_remote_copy(
        src_ref=fin.at[pl.ds(0, DP - 1)], dst_ref=fin.at[pl.ds(0, DP - 1)],
        send_sem=fin_sem.at[0], recv_sem=fin_sem.at[1],
        device_id=(lax.rem(dp + 1, DP), ctx), device_id_type=MESH,
    )
    row.wait_recv()
    row.wait_send()
    for q in range(NX):
        gin_ref[:, q * 128 : (q + 1) * 128] = fin[q]
        gout_ref[:, q * 128 : (q + 1) * 128] = fin[NX + q]

    for copy in swaps + copies + more:
        copy.wait_send()
    for store in stores:
        store.wait()


def on_device(inputs, step_size, decay_rate, frequency, input_proj, output_proj, skip_gain, cotangent):
    vmem = pl.BlockSpec(memory_space=pltpu.VMEM)
    hbm = pl.BlockSpec(memory_space=pl.ANY)
    out, ig, gin, gout = pl.pallas_call(
        kernel,
        out_shape=(
            jax.ShapeDtypeStruct((ROWS, WIDTH), BF16),
            jax.ShapeDtypeStruct((ROWS, WIDTH), BF16),
            jax.ShapeDtypeStruct((WIDTH // PEERS, 2 * STATES), F32),
            jax.ShapeDtypeStruct((WIDTH // PEERS, 2 * STATES), F32),
        ),
        in_specs=[hbm, vmem, vmem, vmem, hbm, hbm, vmem, hbm],
        out_specs=(hbm, hbm, vmem, vmem),
        scratch_shapes=[
            pltpu.VMEM((2, ROWS, WIDTH), BF16),
            pltpu.VMEM((2, WIDTH, 2 * STATES), BF16),
            pltpu.VMEM((2, WIDTH, ROWS), BF16),
            pltpu.VMEM((ROWS, 128), F32),
            pltpu.VMEM((4, ROWS, 128), F32),
            pltpu.VMEM((2, 4, ROWS, 128), F32),
            pltpu.VMEM((2, ROWS, 2 * STATES), BF16),
            pltpu.VMEM((2, ROWS, WIDTH), BF16),
            pltpu.VMEM((20, SUB, 128), F32),
            pltpu.VMEM((2, 8, 128), F32),
            pltpu.VMEM((PEERS, 8, 128), F32),
            pltpu.VMEM((4, 4, NZ, 32, 128), F32),
            pltpu.VMEM((4, 4, NZ, 32, 128), F32),
            pltpu.VMEM((4, 4, NZ, 32, 128), F32),
            pltpu.VMEM((6, 2, NZ, 32, 128), F32),
            pltpu.VMEM((6, 4, 32, 128), F32),
            pltpu.VMEM((NZ, 32, 128), F32),
            pltpu.VMEM((DP, 32, 128), F32),
            pltpu.SemaphoreType.DMA((4,)),
            pltpu.SemaphoreType.DMA((2,)),
            pltpu.SemaphoreType.DMA((2,)),
            pltpu.SemaphoreType.DMA((2, 4)),
            pltpu.SemaphoreType.DMA((2, 2, 6)),
            pltpu.SemaphoreType.DMA((2,)),
            pltpu.SemaphoreType.DMA((2,)),
        ],
        compiler_params=pltpu.CompilerParams(
            collective_id=0, has_side_effects=True, vmem_limit_bytes=56 * 1024 * 1024
        ),
    )(
        inputs.reshape(ROWS, WIDTH), step_size, decay_rate.reshape(1, STATES), frequency.reshape(1, STATES),
        input_proj, output_proj, skip_gain.reshape(1, WIDTH), cotangent.reshape(ROWS, WIDTH),
    )
    return out.reshape(1, ROWS, WIDTH), ig.reshape(1, ROWS, WIDTH), gin, gout


def solution(mesh):
    in_specs = (
        P("dp", "context", None), P("dp", "context"), P(), P(), P(), P(), P(), P("dp", "context", None),
    )
    out_specs = (
        P("dp", "context", None), P("dp", "context", None), P("context", None), P("context", None),
    )
    return jax.shard_map(on_device, mesh=mesh, in_specs=in_specs, out_specs=out_specs, check_vma=False)
```

```python
import jax
import jax.numpy as jnp
from jax import lax
from jax.experimental import pallas as pl
from jax.experimental.pallas import tpu as pltpu
from jax.sharding import PartitionSpec as P

MESH = pl.DeviceIdType.MESH
F32, BF16 = jnp.float32, jnp.bfloat16
ROWS, WIDTH, STATES = 512, 1024, 256
SUB = 8
LAPS = ROWS // SUB
PITCH = LAPS + 1
NX, NY, NZ = 4, 4, 8
PEERS = NY * NZ
DP = 2 * NX
SCALE = float(8 * 16384) ** -0.5


def turn(time, decay, frequency):
    damping = jnp.exp(-(time * decay))
    phase = time * frequency
    n = jnp.floor(phase * 0.6366197723675814 + 0.5)
    r = ((phase - n * 1.5703125) - n * 4.837512969970703125e-4) - n * 7.54978995489188216e-8
    q = n.astype(jnp.int32)
    z = r * r
    sine = r + r * z * (-1.6666654611e-1 + z * (8.3321608736e-3 + z * -1.9515295891e-4))
    cosine = (1.0 - 0.5 * z) + z * z * (
        4.166664568298827e-2 + z * (-1.388731625493765e-3 + z * 2.443315711809948e-5)
    )
    swap = (q & 1) == 1
    a = jnp.where(swap, sine, cosine)
    b = jnp.where(swap, cosine, sine)
    re = jnp.where(((q + 1) & 2) == 2, -a, a)
    im = jnp.where((q & 2) == 2, -b, b)
    return damping * re, damping * im


def cmul(ar, ai, br, bi):
    return ar * br - ai * bi, ar * bi + ai * br


def cmulc(ar, ai, br, bi):
    return ar * br + ai * bi, ar * bi - ai * br


def kernel(
    x_hbm, step_ref, decay_ref, freq_ref, win_hbm, wout_hbm, skip_ref, cot_hbm,
    out_hbm, ig_hbm, gin_ref, gout_ref,
    xc, wio, xct, stb, lam, drv, pairs, outs, chunk, msg, rmsg, own, theirs, partner,
    r1, r2, r3, fin,
    load_sem, store_sem, pre_sem, pair_sem, ring_sem, z_sem, fin_sem,
):
    dp = lax.axis_index("dp")
    ctx = lax.axis_index("context")
    core, x = lax.rem(dp, 2), lax.div(dp, 2)
    y, z = lax.rem(ctx, NY), lax.div(ctx, NY)
    other = 1 - core

    barrier = pltpu.get_barrier_semaphore()

    def greet_context(d, _):
        pl.semaphore_signal(barrier, inc=1, device_id=(dp, lax.rem(ctx + d, PEERS)), device_id_type=MESH)
        return 0

    def greet_dp(d, _):
        pl.semaphore_signal(barrier, inc=1, device_id=(lax.rem(dp + d, DP), ctx), device_id_type=MESH)
        return 0

    loads = [
        pltpu.make_async_copy(x_hbm, xc.at[0], load_sem.at[0]),
        pltpu.make_async_copy(win_hbm, wio.at[0], load_sem.at[1]),
        pltpu.make_async_copy(cot_hbm, xc.at[1], load_sem.at[2]),
        pltpu.make_async_copy(wout_hbm, wio.at[1], load_sem.at[3]),
    ]
    for load in loads:
        load.start()
    lax.fori_loop(1, PEERS, greet_context, 0)
    lax.fori_loop(1, DP, greet_dp, 0)

    decay = [decay_ref[:, g * 128 : (g + 1) * 128] for g in range(2)]
    freq = [freq_ref[:, g * 128 : (g + 1) * 128] for g in range(2)]
    gain = []
    for g in range(2):
        v = 2.0 * decay[g]
        s = jnp.ones_like(v)
        for k in range(9, 1, -1):
            s = 1.0 - v * (1.0 / k) * s
        gain.append(jnp.sqrt(v * s))

    for r in range(ROWS // 128):
        line = jnp.broadcast_to(step_ref[:, r * 128 : (r + 1) * 128], (128, 128))
        turned = line.T
        for s in (0, 1):
            stb[pl.ds((2 * r + s) * PITCH, LAPS), :] = turned[s * LAPS : (s + 1) * LAPS]

    def lam_block(i, _):
        rows = pl.ds(lax.div(i, 2) * PITCH + lax.rem(i, 2) * 32, 32)
        st = stb[rows, :]
        for g in range(2):
            re, im = turn(st, decay[g], freq[g])
            lam[g, rows, :] = re
            lam[2 + g, rows, :] = im
        return 0

    lax.fori_loop(0, ROWS // 32, lam_block, 0)

    for m in range(2):
        loads[2 * m].wait()
        loads[2 * m + 1].wait()
        for nb in range(2):
            res = jnp.dot(xc[m], wio[m, :, nb * 256 : (nb + 1) * 256], preferred_element_type=F32)
            for g in range(2):
                part = res[:, g * 128 : (g + 1) * 128]
                part = part * gain[g] if m == 0 else part
                for s in range(SUB):
                    drv[m, 2 * nb + g, s * PITCH : s * PITCH + LAPS, :] = part[s * LAPS : (s + 1) * LAPS]

    def scan_step(j, carry, store):
        f, b, total = carry[:4], carry[4:8], carry[8]
        rf = pl.ds(j, SUB, stride=PITCH)
        rb = pl.ds(LAPS - 1 - j, SUB, stride=PITCH)
        nf, nb = [None] * 4, [None] * 4
        for g in range(2):
            re, im = cmul(lam[g, rf, :], lam[2 + g, rf, :], f[g], f[2 + g])
            nf[g] = re + drv[0, g, rf, :]
            nf[2 + g] = im + drv[0, 2 + g, rf, :]
            ar = drv[1, g, rb, :] + b[g]
            ai = drv[1, 2 + g, rb, :] + b[2 + g]
            if store:
                drv[0, g, rf, :] = nf[g]
                drv[0, 2 + g, rf, :] = nf[2 + g]
                drv[1, g, rb, :] = ar
                drv[1, 2 + g, rb, :] = ai
            nb[g], nb[2 + g] = cmulc(lam[g, rb, :], lam[2 + g, rb, :], ar, ai)
        if not store:
            total = total + stb[rf, :]
        return (*nf, *nb, total)

    zero = jnp.zeros((SUB, 128), F32)
    summary = lax.fori_loop(0, LAPS, lambda j, c: scan_step(j, c, False), (zero,) * 9)
    for k in range(8):
        chunk[4 + k] = summary[k]
    for g in range(2):
        chunk[g], chunk[2 + g] = turn(jnp.minimum(summary[8], 8.0e6), decay[g], freq[g])
    msg[...] = jnp.zeros_like(msg)

    def pass_chunks(entering, keep):
        f, b = list(entering[:4]), list(entering[4:])
        for s in range(SUB):
            e = SUB - 1 - s
            for g in range(2):
                if keep:
                    for h in (g, 2 + g):
                        chunk[12 + h, s : s + 1, :] = f[h]
                        chunk[16 + h, e : e + 1, :] = b[h]
                re, im = cmul(chunk[g, s : s + 1, :], chunk[2 + g, s : s + 1, :], f[g], f[2 + g])
                f[g] = re + chunk[4 + g, s : s + 1, :]
                f[2 + g] = im + chunk[6 + g, s : s + 1, :]
                re, im = cmulc(chunk[g, e : e + 1, :], chunk[2 + g, e : e + 1, :], b[g], b[2 + g])
                b[g] = re + chunk[8 + g, e : e + 1, :]
                b[2 + g] = im + chunk[10 + g, e : e + 1, :]
        return f + b

    leave = pass_chunks((jnp.zeros((1, 128), F32),) * 8, False)
    total = jnp.sum(summary[8], axis=0, keepdims=True)
    for k in range(4):
        msg[0, k : k + 1, :] = leave[k]
        msg[1, k : k + 1, :] = leave[4 + k]
    msg[0, 4:5, :] = total
    msg[1, 4:5, :] = total
    rmsg[ctx] = jnp.zeros((8, 128), F32)

    pl.semaphore_wait(barrier, PEERS - 1 + DP - 1)

    for dz in (4, 3, 5, 2, 6, 1, 7, 0):
        for dy in (2, 1, 3, 0):
            if dz or dy:
                peer = lax.rem(z + dz, NZ) * NY + lax.rem(y + dy, NY)
                pltpu.make_async_remote_copy(
                    src_ref=msg.at[(peer < ctx).astype(jnp.int32)], dst_ref=rmsg.at[ctx],
                    send_sem=pre_sem.at[0], recv_sem=pre_sem.at[1],
                    device_id=(dp, peer), device_id_type=MESH,
                ).start()

    for m in range(2):
        def turn_block(i, _, m=m):
            cols = pl.ds(pl.multiple_of(i * 128, 128), 128)
            xct[m, cols, :] = xc[m, :, cols].T
            return 0

        lax.fori_loop(0, WIDTH // 128, turn_block, 0)

    everyone = pltpu.make_async_remote_copy(
        src_ref=rmsg.at[pl.ds(0, PEERS - 1)], dst_ref=rmsg.at[pl.ds(0, PEERS - 1)],
        send_sem=pre_sem.at[0], recv_sem=pre_sem.at[1],
        device_id=(dp, lax.rem(ctx + 1, PEERS)), device_id_type=MESH,
    )
    everyone.wait_recv()
    everyone.wait_send()

    place = lax.broadcasted_iota(jnp.int32, (PEERS, 128), 0)
    gap = jnp.zeros((PEERS, 128), F32)
    for i in range(PEERS):
        side = 2 * (i < ctx).astype(jnp.int32) - 1
        gap = gap + jnp.where((i - place) * side > 0, rmsg[i, 4:5, :], 0.0)
    gap = jnp.minimum(gap, 8.0e6)
    sign = jnp.where(place < ctx, 1.0, -1.0)
    entering = [None] * 8
    for g in range(2):
        wr, wi = turn(gap, decay[g], sign * freq[g])
        re, im = cmul(wr, wi, rmsg[:, g, :], rmsg[:, 2 + g, :])
        for h, v in ((g, re), (2 + g, im)):
            entering[h] = jnp.sum(jnp.where(place < ctx, v, 0.0), axis=0, keepdims=True)
            entering[4 + h] = jnp.sum(jnp.where(place > ctx, v, 0.0), axis=0, keepdims=True)
    pass_chunks(entering, True)
    start = tuple(chunk[12 + k] for k in range(8)) + (zero,)
    lax.fori_loop(0, LAPS, lambda j, c: scan_step(j, c, True), start)

    def round_block(i, _):
        rows = pl.ds(pl.multiple_of(i * 32, 32), 32)
        held = pl.ds(lax.div(i, 2) * PITCH + lax.rem(i, 2) * 32, 32)
        for k in range(4):
            pairs[0, rows, k * 128 : (k + 1) * 128] = (drv[1, k, held, :] * gain[k % 2]).astype(BF16)
            pairs[1, rows, k * 128 : (k + 1) * 128] = drv[0, k, held, :].astype(BF16)
        return 0

    lax.fori_loop(0, ROWS // 32, round_block, 0)

    def gradient(m, into):
        def rows_block(i, _):
            rows = pl.ds(pl.multiple_of(i * 256, 256), 256)
            res = jnp.dot(xct[m, rows, :], pairs[m], preferred_element_type=F32)
            for zi in range(2):
                for yy in range(NY):
                    top = (zi * NY + yy) * 32
                    for q in range(NX):
                        a = q + m * (yy - q)
                        b = yy + m * (q - yy)
                        into[a, b, 2 * i + zi] = res[top : top + 32, q * 128 : (q + 1) * 128]
            return 0

        lax.fori_loop(0, WIDTH // 256, rows_block, 0)

    spot = x + core * (y - x)
    spot_other = y + core * (x - y)
    gradient(other, theirs)
    swaps = []
    for k, d in enumerate((2, 1, 3, 0)):
        a = lax.rem(spot_other + d, 4)
        swap = pltpu.make_async_remote_copy(
            src_ref=theirs.at[a], dst_ref=partner.at[k],
            send_sem=pair_sem.at[0, k], recv_sem=pair_sem.at[1, k],
            device_id=(2 * x + other, ctx), device_id_type=MESH,
        )
        swap.start()
        swaps.append(swap)
    gradient(core, own)

    def first_ring(d):
        return (2 * lax.rem(x + other * d, 4) + core, z * NY + lax.rem(y + core * d, 4))

    def second_ring(d):
        return (2 * lax.rem(x + core * d, 4) + core, z * NY + lax.rem(y + other * d, 4))

    def send(src, dst, ring, i, device):
        copy = pltpu.make_async_remote_copy(
            src_ref=src, dst_ref=dst, send_sem=ring_sem.at[ring, 0, i], recv_sem=ring_sem.at[ring, 1, i],
            device_id=device, device_id_type=MESH,
        )
        copy.start()
        return copy

    def take_partner(k, d):
        a = lax.rem(spot + d, 4)
        swaps[k].wait_recv()

        def add(i, _):
            own[a, lax.div(i, 2), pl.ds(lax.rem(i, 2) * 4, 4)] += partner[k, lax.div(i, 2), pl.ds(lax.rem(i, 2) * 4, 4)]
            return 0

        lax.fori_loop(0, 8, add, 0)

    def half1(d, h):
        return own.at[lax.rem(spot + d, 4), pl.ds(2 * h, 2)]

    def half2(d, h):
        return own.at[spot, lax.rem(spot_other + d, 4), pl.ds(4 * h, 4)]

    def add_into(view, buf, blocks):
        def add(i, _):
            if len(view.shape) == 4:
                view[lax.div(i, 8), lax.rem(i, 8)] += buf[lax.div(i, 8), lax.rem(i, 8)]
            else:
                view[i] += buf[i]
            return 0

        lax.fori_loop(0, blocks, add, 0)

    copies = [None] * 6
    take_partner(0, 2)
    copies[0] = send(half1(2, 0), r1.at[0], 0, 0, first_ring(1))
    copies[1] = send(half1(2, 1), r1.at[1], 0, 1, first_ring(3))
    take_partner(1, 1)
    copies[2] = send(half1(1, 1), r1.at[2], 0, 2, first_ring(1))
    take_partner(2, 3)
    copies[3] = send(half1(3, 0), r1.at[3], 0, 3, first_ring(3))
    take_partner(3, 0)

    stores = []
    for m in range(2):
        def out_block(i, _, m=m):
            cols = pl.ds(pl.multiple_of(i * 256, 256), 256)
            mixed = lax.dot_general(
                pairs[1 - m], wio[1 - m, cols, :], (((1,), (1,)), ((), ())), preferred_element_type=F32
            )
            outs[m, :, cols] = (mixed + skip_ref[:, cols] * xc[m, :, cols].astype(F32)).astype(BF16)
            return 0

        lax.fori_loop(0, WIDTH // 256, out_block, 0)
        store = pltpu.make_async_copy(outs.at[m], (out_hbm, ig_hbm)[m], store_sem.at[m])
        store.start()
        stores.append(store)

    copies[0].wait_recv()
    add_into(half1(1, 0), r1.at[0], 16)
    copies[4] = send(half1(1, 0), r1.at[4], 0, 4, first_ring(1))
    copies[1].wait_recv()
    add_into(half1(3, 1), r1.at[1], 16)
    copies[5] = send(half1(3, 1), r1.at[5], 0, 5, first_ring(3))
    copies[3].wait_recv()
    add_into(half1(0, 0), r1.at[3], 16)
    copies[2].wait_recv()
    add_into(half1(0, 1), r1.at[2], 16)
    copies[4].wait_recv()
    add_into(half1(0, 0), r1.at[4], 16)
    copies[5].wait_recv()
    add_into(half1(0, 1), r1.at[5], 16)

    more = [None] * 6
    more[0] = send(half2(2, 0), r2.at[0], 1, 0, second_ring(1))
    more[1] = send(half2(2, 1), r2.at[1], 1, 1, second_ring(3))
    more[2] = send(half2(1, 1), r2.at[2], 1, 2, second_ring(1))
    more[3] = send(half2(3, 0), r2.at[3], 1, 3, second_ring(3))
    more[0].wait_recv()
    add_into(half2(1, 0), r2.at[0], 4)
    more[4] = send(half2(1, 0), r2.at[4], 1, 4, second_ring(1))
    more[1].wait_recv()
    add_into(half2(3, 1), r2.at[1], 4)
    more[5] = send(half2(3, 1), r2.at[5], 1, 5, second_ring(3))
    more[3].wait_recv()
    add_into(half2(0, 0), r2.at[3], 4)
    more[2].wait_recv()
    add_into(half2(0, 1), r2.at[2], 4)
    more[4].wait_recv()
    add_into(half2(0, 0), r2.at[4], 4)
    more[5].wait_recv()
    add_into(half2(0, 1), r2.at[5], 4)

    for dz in (4, 3, 5, 2, 6, 1, 7):
        zz = lax.rem(z + dz, NZ)
        pltpu.make_async_remote_copy(
            src_ref=own.at[spot, spot_other, zz], dst_ref=r3.at[z],
            send_sem=z_sem.at[0], recv_sem=z_sem.at[1],
            device_id=(dp, zz * NY + y), device_id_type=MESH,
        ).start()
    r3[z] = own[spot, spot_other, z]
    column = pltpu.make_async_remote_copy(
        src_ref=r3.at[pl.ds(0, NZ - 1)], dst_ref=r3.at[pl.ds(0, NZ - 1)],
        send_sem=z_sem.at[0], recv_sem=z_sem.at[1],
        device_id=(dp, lax.rem(z + 1, NZ) * NY + y), device_id_type=MESH,
    )
    column.wait_recv()
    column.wait_send()
    piece = r3[0]
    for k in range(1, NZ):
        piece = piece + r3[k]
    mine = core * NX + x
    fin[mine] = piece * SCALE
    for d in (4, 5, 3, 2, 6, 7, 1):
        peer = lax.rem(dp + d, DP)
        pltpu.make_async_remote_copy(
            src_ref=fin.at[mine], dst_ref=fin.at[mine],
            send_sem=fin_sem.at[0], recv_sem=fin_sem.at[1],
            device_id=(peer, ctx), device_id_type=MESH,
        ).start()
    row = pltpu.make_async_remote_copy(
        src_ref=fin.at[pl.ds(0, DP - 1)], dst_ref=fin.at[pl.ds(0, DP - 1)],
        send_sem=fin_sem.at[0], recv_sem=fin_sem.at[1],
        device_id=(lax.rem(dp + 1, DP), ctx), device_id_type=MESH,
    )
    row.wait_recv()
    row.wait_send()
    for q in range(NX):
        gin_ref[:, q * 128 : (q + 1) * 128] = fin[q]
        gout_ref[:, q * 128 : (q + 1) * 128] = fin[NX + q]

    for copy in swaps + copies + more:
        copy.wait_send()
    for store in stores:
        store.wait()


def on_device(inputs, step_size, decay_rate, frequency, input_proj, output_proj, skip_gain, cotangent):
    vmem = pl.BlockSpec(memory_space=pltpu.VMEM)
    hbm = pl.BlockSpec(memory_space=pl.ANY)
    out, ig, gin, gout = pl.pallas_call(
        kernel,
        out_shape=(
            jax.ShapeDtypeStruct((ROWS, WIDTH), BF16),
            jax.ShapeDtypeStruct((ROWS, WIDTH), BF16),
            jax.ShapeDtypeStruct((WIDTH // PEERS, 2 * STATES), F32),
            jax.ShapeDtypeStruct((WIDTH // PEERS, 2 * STATES), F32),
        ),
        in_specs=[hbm, vmem, vmem, vmem, hbm, hbm, vmem, hbm],
        out_specs=(hbm, hbm, vmem, vmem),
        scratch_shapes=[
            pltpu.VMEM((2, ROWS, WIDTH), BF16),
            pltpu.VMEM((2, WIDTH, 2 * STATES), BF16),
            pltpu.VMEM((2, WIDTH, ROWS), BF16),
            pltpu.VMEM((SUB * PITCH, 128), F32),
            pltpu.VMEM((4, SUB * PITCH, 128), F32),
            pltpu.VMEM((2, 4, SUB * PITCH, 128), F32),
            pltpu.VMEM((2, ROWS, 2 * STATES), BF16),
            pltpu.VMEM((2, ROWS, WIDTH), BF16),
            pltpu.VMEM((20, SUB, 128), F32),
            pltpu.VMEM((2, 8, 128), F32),
            pltpu.VMEM((PEERS, 8, 128), F32),
            pltpu.VMEM((4, 4, NZ, 32, 128), F32),
            pltpu.VMEM((4, 4, NZ, 32, 128), F32),
            pltpu.VMEM((4, 4, NZ, 32, 128), F32),
            pltpu.VMEM((6, 2, NZ, 32, 128), F32),
            pltpu.VMEM((6, 4, 32, 128), F32),
            pltpu.VMEM((NZ, 32, 128), F32),
            pltpu.VMEM((DP, 32, 128), F32),
            pltpu.SemaphoreType.DMA((4,)),
            pltpu.SemaphoreType.DMA((2,)),
            pltpu.SemaphoreType.DMA((2,)),
            pltpu.SemaphoreType.DMA((2, 4)),
            pltpu.SemaphoreType.DMA((2, 2, 6)),
            pltpu.SemaphoreType.DMA((2,)),
            pltpu.SemaphoreType.DMA((2,)),
        ],
        compiler_params=pltpu.CompilerParams(
            collective_id=0, has_side_effects=True, vmem_limit_bytes=56 * 1024 * 1024
        ),
    )(
        inputs.reshape(ROWS, WIDTH), step_size, decay_rate.reshape(1, STATES), frequency.reshape(1, STATES),
        input_proj, output_proj, skip_gain.reshape(1, WIDTH), cotangent.reshape(ROWS, WIDTH),
    )
    return out.reshape(1, ROWS, WIDTH), ig.reshape(1, ROWS, WIDTH), gin, gout


def solution(mesh):
    in_specs = (
        P("dp", "context", None), P("dp", "context"), P(), P(), P(), P(), P(), P("dp", "context", None),
    )
    out_specs = (
        P("dp", "context", None), P("dp", "context", None), P("context", None), P("context", None),
    )
    return jax.shard_map(on_device, mesh=mesh, in_specs=in_specs, out_specs=out_specs, check_vma=False)
```

```python
import jax
import jax.numpy as jnp
from jax import lax
from jax.experimental import pallas as pl
from jax.experimental.pallas import tpu as pltpu
from jax.sharding import PartitionSpec as P

MESH = pl.DeviceIdType.MESH
F32, BF16 = jnp.float32, jnp.bfloat16
ROWS, WIDTH, STATES = 512, 1024, 256
SUB = 8
LAPS = ROWS // SUB
PITCH = LAPS + 1
NX, NY, NZ = 4, 4, 8
PEERS = NY * NZ
DP = 2 * NX
PARTS = 4
SCALE = float(8 * 16384) ** -0.5


def turn(time, decay, frequency):
    damping = jnp.exp(-(time * decay))
    phase = time * frequency
    n = jnp.floor(phase * 0.6366197723675814 + 0.5)
    r = ((phase - n * 1.5703125) - n * 4.837512969970703125e-4) - n * 7.54978995489188216e-8
    q = n.astype(jnp.int32)
    z = r * r
    sine = r + r * z * (-1.6666654611e-1 + z * (8.3321608736e-3 + z * -1.9515295891e-4))
    cosine = (1.0 - 0.5 * z) + z * z * (
        4.166664568298827e-2 + z * (-1.388731625493765e-3 + z * 2.443315711809948e-5)
    )
    swap = (q & 1) == 1
    a = jnp.where(swap, sine, cosine)
    b = jnp.where(swap, cosine, sine)
    re = jnp.where(((q + 1) & 2) == 2, -a, a)
    im = jnp.where((q & 2) == 2, -b, b)
    return damping * re, damping * im


def cmul(ar, ai, br, bi):
    return ar * br - ai * bi, ar * bi + ai * br


def cmulc(ar, ai, br, bi):
    return ar * br + ai * bi, ar * bi - ai * br


def kernel(
    x_hbm, step_ref, decay_ref, freq_ref, win_hbm, wout_hbm, skip_ref, cot_hbm,
    out_ref, ig_ref, gin_ref, gout_ref,
    xc, wio, xct, stb, lam, drv, pairs, chunk, msg, rmsg, own, theirs, partner,
    r1, r2, up, r3, fin,
    load_sem, pre_sem, pair_sem, ring_sem, second_sem, z_sem, fin_sem,
):
    dp = lax.axis_index("dp")
    ctx = lax.axis_index("context")
    core, x = lax.rem(dp, 2), lax.div(dp, 2)
    y, z = lax.rem(ctx, NY), lax.div(ctx, NY)
    other = 1 - core

    barrier = pltpu.get_barrier_semaphore()

    def greet_context(d, _):
        pl.semaphore_signal(barrier, inc=1, device_id=(dp, lax.rem(ctx + d, PEERS)), device_id_type=MESH)
        return 0

    def greet_dp(d, _):
        pl.semaphore_signal(barrier, inc=1, device_id=(lax.rem(dp + d, DP), ctx), device_id_type=MESH)
        return 0

    loads = [
        pltpu.make_async_copy(x_hbm, xc.at[0], load_sem.at[0]),
        pltpu.make_async_copy(win_hbm, wio.at[0], load_sem.at[1]),
        pltpu.make_async_copy(cot_hbm, xc.at[1], load_sem.at[2]),
        pltpu.make_async_copy(wout_hbm, wio.at[1], load_sem.at[3]),
    ]
    for load in loads:
        load.start()
    lax.fori_loop(1, PEERS, greet_context, 0)
    lax.fori_loop(1, DP, greet_dp, 0)

    decay = [decay_ref[:, g * 128 : (g + 1) * 128] for g in range(2)]
    freq = [freq_ref[:, g * 128 : (g + 1) * 128] for g in range(2)]
    gain = []
    for g in range(2):
        v = 2.0 * decay[g]
        s = jnp.ones_like(v)
        for k in range(9, 1, -1):
            s = 1.0 - v * (1.0 / k) * s
        gain.append(jnp.sqrt(v * s))

    for r in range(ROWS // 128):
        line = jnp.broadcast_to(step_ref[:, r * 128 : (r + 1) * 128], (128, 128))
        turned = line.T
        for s in (0, 1):
            stb[pl.ds((2 * r + s) * PITCH, LAPS), :] = turned[s * LAPS : (s + 1) * LAPS]

    def lam_block(i, _):
        rows = pl.ds(lax.div(i, 2) * PITCH + lax.rem(i, 2) * 32, 32)
        st = stb[rows, :]
        for g in range(2):
            re, im = turn(st, decay[g], freq[g])
            lam[g, rows, :] = re
            lam[2 + g, rows, :] = im
        return 0

    lax.fori_loop(0, ROWS // 32, lam_block, 0)

    for m in range(2):
        loads[2 * m].wait()
        loads[2 * m + 1].wait()
        for nb in range(2):
            res = jnp.dot(xc[m], wio[m, :, nb * 256 : (nb + 1) * 256], preferred_element_type=F32)
            for g in range(2):
                part = res[:, g * 128 : (g + 1) * 128]
                part = part * gain[g] if m == 0 else part
                for s in range(SUB):
                    drv[m, 2 * nb + g, s * PITCH : s * PITCH + LAPS, :] = part[s * LAPS : (s + 1) * LAPS]

    def scan_step(j, carry, store):
        f, b, total = carry[:4], carry[4:8], carry[8]
        rf = pl.ds(j, SUB, stride=PITCH)
        rb = pl.ds(LAPS - 1 - j, SUB, stride=PITCH)
        nf, nb = [None] * 4, [None] * 4
        for g in range(2):
            re, im = cmul(lam[g, rf, :], lam[2 + g, rf, :], f[g], f[2 + g])
            nf[g] = re + drv[0, g, rf, :]
            nf[2 + g] = im + drv[0, 2 + g, rf, :]
            ar = drv[1, g, rb, :] + b[g]
            ai = drv[1, 2 + g, rb, :] + b[2 + g]
            if store:
                drv[0, g, rf, :] = nf[g]
                drv[0, 2 + g, rf, :] = nf[2 + g]
                drv[1, g, rb, :] = ar
                drv[1, 2 + g, rb, :] = ai
            nb[g], nb[2 + g] = cmulc(lam[g, rb, :], lam[2 + g, rb, :], ar, ai)
        if not store:
            total = total + stb[rf, :]
        return (*nf, *nb, total)

    zero = jnp.zeros((SUB, 128), F32)
    summary = lax.fori_loop(0, LAPS, lambda j, c: scan_step(j, c, False), (zero,) * 9)
    for k in range(8):
        chunk[4 + k] = summary[k]
    for g in range(2):
        chunk[g], chunk[2 + g] = turn(jnp.minimum(summary[8], 8.0e6), decay[g], freq[g])
    msg[...] = jnp.zeros_like(msg)

    def pass_chunks(entering, keep):
        f, b = list(entering[:4]), list(entering[4:])
        for s in range(SUB):
            e = SUB - 1 - s
            for g in range(2):
                if keep:
                    for h in (g, 2 + g):
                        chunk[12 + h, s : s + 1, :] = f[h]
                        chunk[16 + h, e : e + 1, :] = b[h]
                re, im = cmul(chunk[g, s : s + 1, :], chunk[2 + g, s : s + 1, :], f[g], f[2 + g])
                f[g] = re + chunk[4 + g, s : s + 1, :]
                f[2 + g] = im + chunk[6 + g, s : s + 1, :]
                re, im = cmulc(chunk[g, e : e + 1, :], chunk[2 + g, e : e + 1, :], b[g], b[2 + g])
                b[g] = re + chunk[8 + g, e : e + 1, :]
                b[2 + g] = im + chunk[10 + g, e : e + 1, :]
        return f + b

    leave = pass_chunks((jnp.zeros((1, 128), F32),) * 8, False)
    total = jnp.sum(summary[8], axis=0, keepdims=True)
    for k in range(4):
        msg[0, k : k + 1, :] = leave[k]
        msg[1, k : k + 1, :] = leave[4 + k]
    msg[0, 4:5, :] = total
    msg[1, 4:5, :] = total
    rmsg[ctx] = jnp.zeros((8, 128), F32)

    pl.semaphore_wait(barrier, PEERS - 1 + DP - 1)

    for dz in (4, 3, 5, 2, 6, 1, 7, 0):
        for dy in (2, 1, 3, 0):
            if dz or dy:
                peer = lax.rem(z + dz, NZ) * NY + lax.rem(y + dy, NY)
                pltpu.make_async_remote_copy(
                    src_ref=msg.at[(peer < ctx).astype(jnp.int32)], dst_ref=rmsg.at[ctx],
                    send_sem=pre_sem.at[0], recv_sem=pre_sem.at[1],
                    device_id=(dp, peer), device_id_type=MESH,
                ).start()

    for m in range(2):
        def turn_block(i, _, m=m):
            cols = pl.ds(pl.multiple_of(i * 128, 128), 128)
            xct[m, cols, :] = xc[m, :, cols].T
            return 0

        lax.fori_loop(0, WIDTH // 128, turn_block, 0)

    everyone = pltpu.make_async_remote_copy(
        src_ref=rmsg.at[pl.ds(0, PEERS - 1)], dst_ref=rmsg.at[pl.ds(0, PEERS - 1)],
        send_sem=pre_sem.at[0], recv_sem=pre_sem.at[1],
        device_id=(dp, lax.rem(ctx + 1, PEERS)), device_id_type=MESH,
    )
    everyone.wait_recv()
    everyone.wait_send()

    place = lax.broadcasted_iota(jnp.int32, (PEERS, 128), 0)
    gap = jnp.zeros((PEERS, 128), F32)
    for i in range(PEERS):
        side = 2 * (i < ctx).astype(jnp.int32) - 1
        gap = gap + jnp.where((i - place) * side > 0, rmsg[i, 4:5, :], 0.0)
    gap = jnp.minimum(gap, 8.0e6)
    sign = jnp.where(place < ctx, 1.0, -1.0)
    entering = [None] * 8
    for g in range(2):
        wr, wi = turn(gap, decay[g], sign * freq[g])
        re, im = cmul(wr, wi, rmsg[:, g, :], rmsg[:, 2 + g, :])
        for h, v in ((g, re), (2 + g, im)):
            entering[h] = jnp.sum(jnp.where(place < ctx, v, 0.0), axis=0, keepdims=True)
            entering[4 + h] = jnp.sum(jnp.where(place > ctx, v, 0.0), axis=0, keepdims=True)
    pass_chunks(entering, True)
    start = tuple(chunk[12 + k] for k in range(8)) + (zero,)
    lax.fori_loop(0, LAPS, lambda j, c: scan_step(j, c, True), start)

    def round_block(i, _):
        rows = pl.ds(pl.multiple_of(i * 32, 32), 32)
        held = pl.ds(lax.div(i, 2) * PITCH + lax.rem(i, 2) * 32, 32)
        for k in range(4):
            pairs[0, rows, k * 128 : (k + 1) * 128] = (drv[1, k, held, :] * gain[k % 2]).astype(BF16)
            pairs[1, rows, k * 128 : (k + 1) * 128] = drv[0, k, held, :].astype(BF16)
        return 0

    lax.fori_loop(0, ROWS // 32, round_block, 0)

    def gradient(m, into, then=None):
        def rows_block(i, _):
            rows = pl.ds(pl.multiple_of(i * 256, 256), 256)
            res = jnp.dot(xct[m, rows, :], pairs[m], preferred_element_type=F32)
            for zi in range(2):
                for yy in range(NY):
                    top = (zi * NY + yy) * 32
                    for q in range(NX):
                        a = q + m * (yy - q)
                        b = yy + m * (q - yy)
                        into[i, a, b, zi] = res[top : top + 32, q * 128 : (q + 1) * 128]
            if then is not None:
                then(i)
            return 0

        lax.fori_loop(0, PARTS, rows_block, 0)

    spot = x + core * (y - x)
    spot_other = y + core * (x - y)

    def swap(i):
        return pltpu.make_async_remote_copy(
            src_ref=theirs.at[i], dst_ref=partner.at[i],
            send_sem=pair_sem.at[0, i], recv_sem=pair_sem.at[1, i],
            device_id=(2 * x + other, ctx), device_id_type=MESH,
        )

    gradient(other, theirs, lambda i: swap(i).start())
    gradient(core, own)

    def first_ring(d):
        return (2 * lax.rem(x + other * d, 4) + core, z * NY + lax.rem(y + core * d, 4))

    def second_ring(d):
        return (2 * lax.rem(x + core * d, 4) + core, z * NY + lax.rem(y + other * d, 4))

    def half(i, d, h):
        return own.at[i, lax.rem(spot + d, 4), pl.ds(2 * h, 2)]

    def add_into(view, *bufs):
        total = view[...]
        for buf in bufs:
            total = total + buf[...]
        view[...] = total

    sent = []

    def send_first(i, slot, src, d):
        copy = pltpu.make_async_remote_copy(
            src_ref=src, dst_ref=r1.at[i, slot], send_sem=ring_sem.at[0, i, slot], recv_sem=ring_sem.at[1, i, slot],
            device_id=first_ring(d), device_id_type=MESH,
        )
        copy.start()
        sent.append(copy)
        return copy

    firsts = [[None] * 6 for _ in range(PARTS)]
    seconds = [None] * PARTS

    def begin(i):
        swap(i).wait_recv()

        def add(a, _):
            own[i, a] += partner[i, a]
            return 0

        lax.fori_loop(0, 4, add, 0)
        firsts[i][0] = send_first(i, 0, half(i, 2, 0), 1)
        firsts[i][1] = send_first(i, 1, half(i, 2, 1), 3)
        firsts[i][2] = send_first(i, 2, half(i, 1, 1), 1)
        firsts[i][3] = send_first(i, 3, half(i, 3, 0), 3)

    def relay(i):
        firsts[i][0].wait_recv()
        add_into(half(i, 1, 0), r1.at[i, 0])
        firsts[i][4] = send_first(i, 4, half(i, 1, 0), 1)
        firsts[i][1].wait_recv()
        add_into(half(i, 3, 1), r1.at[i, 1])
        firsts[i][5] = send_first(i, 5, half(i, 3, 1), 3)

    def turn_corner(i):
        for slot in (2, 3, 4, 5):
            firsts[i][slot].wait_recv()
        add_into(half(i, 0, 0), r1.at[i, 3], r1.at[i, 4])
        add_into(half(i, 0, 1), r1.at[i, 2], r1.at[i, 5])
        seconds[i] = []
        for d in (2, 1, 3):
            copy = pltpu.make_async_remote_copy(
                src_ref=own.at[i, spot, lax.rem(spot_other + d, 4)], dst_ref=r2.at[i, d - 1],
                send_sem=second_sem.at[0, i, d - 1], recv_sem=second_sem.at[1, i, d - 1],
                device_id=second_ring(d), device_id_type=MESH,
            )
            copy.start()
            sent.append(copy)
            seconds[i].append(copy)

    def climb(i):
        for copy in seconds[i]:
            copy.wait_recv()
        up[i] = own[i, spot, spot_other] + r2[i, 0] + r2[i, 1] + r2[i, 2]
        for k in range(2):
            goal = 2 * i + k

            @pl.when(z == goal)
            def _():
                r3[z] = up[i, k]

            @pl.when(z != goal)
            def _():
                pltpu.make_async_remote_copy(
                    src_ref=up.at[i, k], dst_ref=r3.at[z],
                    send_sem=z_sem.at[0], recv_sem=z_sem.at[1],
                    device_id=(dp, goal * NY + y), device_id_type=MESH,
                ).start()

    def out_block(m, i):
        cols = slice(i * 256, (i + 1) * 256)
        mixed = lax.dot_general(
            pairs[1 - m], wio[1 - m, cols, :], (((1,), (1,)), ((), ())), preferred_element_type=F32
        )
        (out_ref, ig_ref)[m][:, cols] = (mixed + skip_ref[:, cols] * xc[m, :, cols].astype(F32)).astype(BF16)

    begin(0)
    out_block(0, 0)
    out_block(0, 1)
    begin(1)
    out_block(0, 2)
    out_block(0, 3)
    begin(2)
    out_block(1, 0)
    relay(0)
    begin(3)
    out_block(1, 1)
    relay(1)
    turn_corner(0)
    out_block(1, 2)
    relay(2)
    turn_corner(1)
    climb(0)
    out_block(1, 3)
    relay(3)
    turn_corner(2)
    climb(1)
    turn_corner(3)
    climb(2)
    climb(3)

    column = pltpu.make_async_remote_copy(
        src_ref=r3.at[pl.ds(0, NZ - 1)], dst_ref=r3.at[pl.ds(0, NZ - 1)],
        send_sem=z_sem.at[0], recv_sem=z_sem.at[1],
        device_id=(dp, lax.rem(z + 1, NZ) * NY + y), device_id_type=MESH,
    )
    column.wait_recv()
    piece = r3[0]
    for k in range(1, NZ):
        piece = piece + r3[k]
    mine = core * NX + x
    fin[mine] = piece * SCALE
    for d in (4, 5, 3, 2, 6, 7, 1):
        pltpu.make_async_remote_copy(
            src_ref=fin.at[mine], dst_ref=fin.at[mine],
            send_sem=fin_sem.at[0], recv_sem=fin_sem.at[1],
            device_id=(lax.rem(dp + d, DP), ctx), device_id_type=MESH,
        ).start()
    row = pltpu.make_async_remote_copy(
        src_ref=fin.at[pl.ds(0, DP - 1)], dst_ref=fin.at[pl.ds(0, DP - 1)],
        send_sem=fin_sem.at[0], recv_sem=fin_sem.at[1],
        device_id=(lax.rem(dp + 1, DP), ctx), device_id_type=MESH,
    )
    column.wait_send()
    for i in range(PARTS):
        swap(i).wait_send()
    for copy in sent:
        copy.wait_send()
    row.wait_recv()
    for q in range(NX):
        gin_ref[:, q * 128 : (q + 1) * 128] = fin[q]
        gout_ref[:, q * 128 : (q + 1) * 128] = fin[NX + q]
    row.wait_send()


def store_kernel(*refs):
    sems = refs[8]
    copies = [pltpu.make_async_copy(refs[k], refs[4 + k], sems.at[k]) for k in range(4)]
    for copy in copies:
        copy.start()
    for copy in copies:
        copy.wait()


def on_device(inputs, step_size, decay_rate, frequency, input_proj, output_proj, skip_gain, cotangent):
    vmem = pl.BlockSpec(memory_space=pltpu.VMEM)
    hbm = pl.BlockSpec(memory_space=pltpu.HBM)
    results = [((ROWS, WIDTH), BF16)] * 2 + [((WIDTH // PEERS, 2 * STATES), F32)] * 2
    held = pl.pallas_call(
        kernel,
        out_shape=tuple(pltpu.VMEM(shape, dtype) for shape, dtype in results),
        in_specs=[hbm, vmem, vmem, vmem, hbm, hbm, vmem, hbm],
        out_specs=(vmem,) * 4,
        scratch_shapes=[
            pltpu.VMEM((2, ROWS, WIDTH), BF16),
            pltpu.VMEM((2, WIDTH, 2 * STATES), BF16),
            pltpu.VMEM((2, WIDTH, ROWS), BF16),
            pltpu.VMEM((SUB * PITCH, 128), F32),
            pltpu.VMEM((4, SUB * PITCH, 128), F32),
            pltpu.VMEM((2, 4, SUB * PITCH, 128), F32),
            pltpu.VMEM((2, ROWS, 2 * STATES), BF16),
            pltpu.VMEM((20, SUB, 128), F32),
            pltpu.VMEM((2, 8, 128), F32),
            pltpu.VMEM((PEERS, 8, 128), F32),
            pltpu.VMEM((PARTS, 4, 4, 2, 32, 128), F32),
            pltpu.VMEM((PARTS, 4, 4, 2, 32, 128), F32),
            pltpu.VMEM((PARTS, 4, 4, 2, 32, 128), F32),
            pltpu.VMEM((PARTS, 6, 2, 2, 32, 128), F32),
            pltpu.VMEM((PARTS, 3, 2, 32, 128), F32),
            pltpu.VMEM((PARTS, 2, 32, 128), F32),
            pltpu.VMEM((NZ, 32, 128), F32),
            pltpu.VMEM((DP, 32, 128), F32),
            pltpu.SemaphoreType.DMA((4,)),
            pltpu.SemaphoreType.DMA((2,)),
            pltpu.SemaphoreType.DMA((2, PARTS)),
            pltpu.SemaphoreType.DMA((2, PARTS, 6)),
            pltpu.SemaphoreType.DMA((2, PARTS, 3)),
            pltpu.SemaphoreType.DMA((2,)),
            pltpu.SemaphoreType.DMA((2,)),
        ],
        compiler_params=pltpu.CompilerParams(
            collective_id=0, has_side_effects=True, vmem_limit_bytes=60 * 1024 * 1024
        ),
    )(
        inputs.reshape(ROWS, WIDTH), step_size, decay_rate.reshape(1, STATES), frequency.reshape(1, STATES),
        input_proj, output_proj, skip_gain.reshape(1, WIDTH), cotangent.reshape(ROWS, WIDTH),
    )
    out, ig, gin, gout = pl.pallas_call(
        store_kernel,
        out_shape=tuple(jax.ShapeDtypeStruct(shape, dtype) for shape, dtype in results),
        in_specs=[vmem] * 4,
        out_specs=(hbm,) * 4,
        scratch_shapes=[pltpu.SemaphoreType.DMA((4,))],
    )(*(pltpu.with_memory_space_constraint(part, pltpu.VMEM) for part in held))
    return out.reshape(1, ROWS, WIDTH), ig.reshape(1, ROWS, WIDTH), gin, gout


def solution(mesh):
    in_specs = (
        P("dp", "context", None), P("dp", "context"), P(), P(), P(), P(), P(), P("dp", "context", None),
    )
    out_specs = (
        P("dp", "context", None), P("dp", "context", None), P("context", None), P("context", None),
    )
    return jax.shard_map(on_device, mesh=mesh, in_specs=in_specs, out_specs=out_specs, check_vma=False)
```

```python
import jax
import jax.numpy as jnp
from jax import lax
from jax.experimental import pallas as pl
from jax.experimental.pallas import tpu as pltpu
from jax.sharding import PartitionSpec as P

MESH = pl.DeviceIdType.MESH
F32, BF16 = jnp.float32, jnp.bfloat16
ROWS, WIDTH, STATES = 512, 1024, 256
SUB = 8
LAPS = ROWS // SUB
PITCH = LAPS + 1
NX, NY, NZ = 4, 4, 8
PEERS = NY * NZ
DP = 2 * NX
PARTS = 4
SCALE = float(8 * 16384) ** -0.5


def turn(time, decay, frequency):
    damping = jnp.exp(-(time * decay))
    phase = time * frequency
    n = jnp.floor(phase * 0.6366197723675814 + 0.5)
    r = ((phase - n * 1.5703125) - n * 4.837512969970703125e-4) - n * 7.54978995489188216e-8
    q = n.astype(jnp.int32)
    z = r * r
    sine = r + r * z * (-1.6666654611e-1 + z * (8.3321608736e-3 + z * -1.9515295891e-4))
    cosine = (1.0 - 0.5 * z) + z * z * (
        4.166664568298827e-2 + z * (-1.388731625493765e-3 + z * 2.443315711809948e-5)
    )
    swap = (q & 1) == 1
    a = jnp.where(swap, sine, cosine)
    b = jnp.where(swap, cosine, sine)
    re = jnp.where(((q + 1) & 2) == 2, -a, a)
    im = jnp.where((q & 2) == 2, -b, b)
    return damping * re, damping * im


def cmul(ar, ai, br, bi):
    return ar * br - ai * bi, ar * bi + ai * br


def cmulc(ar, ai, br, bi):
    return ar * br + ai * bi, ar * bi - ai * br


def kernel(
    x_hbm, step_hbm, decay_hbm, freq_hbm, win_hbm, wout_hbm, skip_hbm, cot_hbm,
    out_ref, ig_ref, gin_ref, gout_ref,
    step_ref, decay_ref, freq_ref, skip_ref, xc, wio, xct, stb, lam, drv, pairs, chunk, msg, rmsg, own, theirs, partner,
    r1, r2, up, r3, fin,
    small_sem, load_sem, pre_sem, pair_sem, ring_sem, second_sem, z_sem, fin_sem,
):
    dp = lax.axis_index("dp")
    ctx = lax.axis_index("context")
    core, x = lax.rem(dp, 2), lax.div(dp, 2)
    y, z = lax.rem(ctx, NY), lax.div(ctx, NY)
    other = 1 - core

    barrier = pltpu.get_barrier_semaphore()

    def greet_context(d, _):
        pl.semaphore_signal(barrier, inc=1, device_id=(dp, lax.rem(ctx + d, PEERS)), device_id_type=MESH)
        return 0

    def greet_dp(d, _):
        pl.semaphore_signal(barrier, inc=1, device_id=(lax.rem(dp + d, DP), ctx), device_id_type=MESH)
        return 0

    small = [
        pltpu.make_async_copy(src, dst, small_sem.at[k])
        for k, (src, dst) in enumerate(
            ((step_hbm, step_ref), (decay_hbm, decay_ref), (freq_hbm, freq_ref), (skip_hbm, skip_ref))
        )
    ]
    loads = [
        pltpu.make_async_copy(x_hbm, xc.at[0], load_sem.at[0]),
        pltpu.make_async_copy(win_hbm, wio.at[0], load_sem.at[1]),
        pltpu.make_async_copy(cot_hbm, xc.at[1], load_sem.at[2]),
        pltpu.make_async_copy(wout_hbm, wio.at[1], load_sem.at[3]),
    ]
    for load in small + loads:
        load.start()
    lax.fori_loop(1, PEERS, greet_context, 0)
    lax.fori_loop(1, DP, greet_dp, 0)

    for load in small:
        load.wait()
    decay = [decay_ref[:, g * 128 : (g + 1) * 128] for g in range(2)]
    freq = [freq_ref[:, g * 128 : (g + 1) * 128] for g in range(2)]
    gain = []
    for g in range(2):
        v = 2.0 * decay[g]
        s = jnp.ones_like(v)
        for k in range(9, 1, -1):
            s = 1.0 - v * (1.0 / k) * s
        gain.append(jnp.sqrt(v * s))

    for r in range(ROWS // 128):
        line = jnp.broadcast_to(step_ref[:, r * 128 : (r + 1) * 128], (128, 128))
        turned = line.T
        for s in (0, 1):
            stb[pl.ds((2 * r + s) * PITCH, LAPS), :] = turned[s * LAPS : (s + 1) * LAPS]

    def lam_block(i, _):
        rows = pl.ds(lax.div(i, 2) * PITCH + lax.rem(i, 2) * 32, 32)
        st = stb[rows, :]
        for g in range(2):
            re, im = turn(st, decay[g], freq[g])
            lam[g, rows, :] = re
            lam[2 + g, rows, :] = im
        return 0

    lax.fori_loop(0, ROWS // 32, lam_block, 0)

    for m in range(2):
        loads[2 * m].wait()
        loads[2 * m + 1].wait()
        for nb in range(2):
            res = jnp.dot(xc[m], wio[m, :, nb * 256 : (nb + 1) * 256], preferred_element_type=F32)
            for g in range(2):
                part = res[:, g * 128 : (g + 1) * 128]
                part = part * gain[g] if m == 0 else part
                for s in range(SUB):
                    drv[m, 2 * nb + g, s * PITCH : s * PITCH + LAPS, :] = part[s * LAPS : (s + 1) * LAPS]

    def scan_step(j, carry, store):
        f, b, total = carry[:4], carry[4:8], carry[8]
        rf = pl.ds(j, SUB, stride=PITCH)
        rb = pl.ds(LAPS - 1 - j, SUB, stride=PITCH)
        nf, nb = [None] * 4, [None] * 4
        for g in range(2):
            re, im = cmul(lam[g, rf, :], lam[2 + g, rf, :], f[g], f[2 + g])
            nf[g] = re + drv[0, g, rf, :]
            nf[2 + g] = im + drv[0, 2 + g, rf, :]
            ar = drv[1, g, rb, :] + b[g]
            ai = drv[1, 2 + g, rb, :] + b[2 + g]
            if store:
                drv[0, g, rf, :] = nf[g]
                drv[0, 2 + g, rf, :] = nf[2 + g]
                drv[1, g, rb, :] = ar
                drv[1, 2 + g, rb, :] = ai
            nb[g], nb[2 + g] = cmulc(lam[g, rb, :], lam[2 + g, rb, :], ar, ai)
        if not store:
            total = total + stb[rf, :]
        return (*nf, *nb, total)

    zero = jnp.zeros((SUB, 128), F32)
    summary = lax.fori_loop(0, LAPS, lambda j, c: scan_step(j, c, False), (zero,) * 9, unroll=4)
    for k in range(8):
        chunk[4 + k] = summary[k]
    for g in range(2):
        chunk[g], chunk[2 + g] = turn(jnp.minimum(summary[8], 8.0e6), decay[g], freq[g])
    msg[...] = jnp.zeros_like(msg)

    def pass_chunks(entering, keep):
        f, b = list(entering[:4]), list(entering[4:])
        for s in range(SUB):
            e = SUB - 1 - s
            for g in range(2):
                if keep:
                    for h in (g, 2 + g):
                        chunk[12 + h, s : s + 1, :] = f[h]
                        chunk[16 + h, e : e + 1, :] = b[h]
                re, im = cmul(chunk[g, s : s + 1, :], chunk[2 + g, s : s + 1, :], f[g], f[2 + g])
                f[g] = re + chunk[4 + g, s : s + 1, :]
                f[2 + g] = im + chunk[6 + g, s : s + 1, :]
                re, im = cmulc(chunk[g, e : e + 1, :], chunk[2 + g, e : e + 1, :], b[g], b[2 + g])
                b[g] = re + chunk[8 + g, e : e + 1, :]
                b[2 + g] = im + chunk[10 + g, e : e + 1, :]
        return f + b

    leave = pass_chunks((jnp.zeros((1, 128), F32),) * 8, False)
    total = jnp.sum(summary[8], axis=0, keepdims=True)
    for k in range(4):
        msg[0, k : k + 1, :] = leave[k]
        msg[1, k : k + 1, :] = leave[4 + k]
    msg[0, 4:5, :] = total
    msg[1, 4:5, :] = total
    rmsg[ctx] = jnp.zeros((8, 128), F32)

    pl.semaphore_wait(barrier, PEERS - 1 + DP - 1)

    for dz in (4, 3, 5, 2, 6, 1, 7, 0):
        for dy in (2, 1, 3, 0):
            if dz or dy:
                peer = lax.rem(z + dz, NZ) * NY + lax.rem(y + dy, NY)
                pltpu.make_async_remote_copy(
                    src_ref=msg.at[(peer < ctx).astype(jnp.int32), pl.ds(0, 5)], dst_ref=rmsg.at[ctx, pl.ds(0, 5)],
                    send_sem=pre_sem.at[0], recv_sem=pre_sem.at[1],
                    device_id=(dp, peer), device_id_type=MESH,
                ).start()

    for m in range(2):
        def turn_block(i, _, m=m):
            cols = pl.ds(pl.multiple_of(i * 128, 128), 128)
            xct[m, cols, :] = xc[m, :, cols].T
            return 0

        lax.fori_loop(0, WIDTH // 128, turn_block, 0)

    everyone = pltpu.make_async_remote_copy(
        src_ref=rmsg.at[pl.ds(0, PEERS - 1), pl.ds(0, 5)], dst_ref=rmsg.at[pl.ds(0, PEERS - 1), pl.ds(0, 5)],
        send_sem=pre_sem.at[0], recv_sem=pre_sem.at[1],
        device_id=(dp, lax.rem(ctx + 1, PEERS)), device_id_type=MESH,
    )
    everyone.wait_recv()
    everyone.wait_send()

    place = lax.broadcasted_iota(jnp.int32, (PEERS, 128), 0)
    gap = jnp.zeros((PEERS, 128), F32)
    for i in range(PEERS):
        side = 2 * (i < ctx).astype(jnp.int32) - 1
        gap = gap + jnp.where((i - place) * side > 0, rmsg[i, 4:5, :], 0.0)
    gap = jnp.minimum(gap, 8.0e6)
    sign = jnp.where(place < ctx, 1.0, -1.0)
    entering = [None] * 8
    for g in range(2):
        wr, wi = turn(gap, decay[g], sign * freq[g])
        re, im = cmul(wr, wi, rmsg[:, g, :], rmsg[:, 2 + g, :])
        for h, v in ((g, re), (2 + g, im)):
            entering[h] = jnp.sum(jnp.where(place < ctx, v, 0.0), axis=0, keepdims=True)
            entering[4 + h] = jnp.sum(jnp.where(place > ctx, v, 0.0), axis=0, keepdims=True)
    pass_chunks(entering, True)
    start = tuple(chunk[12 + k] for k in range(8)) + (zero,)
    lax.fori_loop(0, LAPS, lambda j, c: scan_step(j, c, True), start, unroll=4)

    def round_block(i, _):
        rows = pl.ds(pl.multiple_of(i * 32, 32), 32)
        held = pl.ds(lax.div(i, 2) * PITCH + lax.rem(i, 2) * 32, 32)
        for k in range(4):
            pairs[0, rows, k * 128 : (k + 1) * 128] = (drv[1, k, held, :] * gain[k % 2]).astype(BF16)
            pairs[1, rows, k * 128 : (k + 1) * 128] = drv[0, k, held, :].astype(BF16)
        return 0

    lax.fori_loop(0, ROWS // 32, round_block, 0)

    def gradient(m, into, then=None):
        def rows_block(i, _):
            rows = pl.ds(pl.multiple_of(i * 256, 256), 256)
            res = jnp.dot(xct[m, rows, :], pairs[m], preferred_element_type=F32)
            for zi in range(2):
                for yy in range(NY):
                    top = (zi * NY + yy) * 32
                    for q in range(NX):
                        a = q + m * (yy - q)
                        b = yy + m * (q - yy)
                        into[i, a, b, zi] = res[top : top + 32, q * 128 : (q + 1) * 128]
            if then is not None:
                then(i)
            return 0

        lax.fori_loop(0, PARTS, rows_block, 0)

    spot = x + core * (y - x)
    spot_other = y + core * (x - y)

    def swap(i):
        return pltpu.make_async_remote_copy(
            src_ref=theirs.at[i], dst_ref=partner.at[i],
            send_sem=pair_sem.at[0, i], recv_sem=pair_sem.at[1, i],
            device_id=(2 * x + other, ctx), device_id_type=MESH,
        )

    gradient(other, theirs, lambda i: swap(i).start())
    gradient(core, own)

    def first_ring(d):
        return (2 * lax.rem(x + other * d, 4) + core, z * NY + lax.rem(y + core * d, 4))

    def second_ring(d):
        return (2 * lax.rem(x + core * d, 4) + core, z * NY + lax.rem(y + other * d, 4))

    def half(i, d, h):
        return own.at[i, lax.rem(spot + d, 4), pl.ds(2 * h, 2)]

    def add_into(view, *bufs):
        total = view[...]
        for buf in bufs:
            total = total + buf[...]
        view[...] = total

    sent = []

    def send_first(i, slot, src, d):
        copy = pltpu.make_async_remote_copy(
            src_ref=src, dst_ref=r1.at[i, slot], send_sem=ring_sem.at[0, i, slot], recv_sem=ring_sem.at[1, i, slot],
            device_id=first_ring(d), device_id_type=MESH,
        )
        copy.start()
        sent.append(copy)
        return copy

    firsts = [[None] * 6 for _ in range(PARTS)]
    seconds = [None] * PARTS

    def begin(i):
        swap(i).wait_recv()

        def add(a, _):
            own[i, a] += partner[i, a]
            return 0

        lax.fori_loop(0, 4, add, 0)
        firsts[i][0] = send_first(i, 0, half(i, 2, 0), 1)
        firsts[i][1] = send_first(i, 1, half(i, 2, 1), 3)
        firsts[i][2] = send_first(i, 2, half(i, 1, 1), 1)
        firsts[i][3] = send_first(i, 3, half(i, 3, 0), 3)

    def relay(i):
        firsts[i][0].wait_recv()
        add_into(half(i, 1, 0), r1.at[i, 0])
        firsts[i][4] = send_first(i, 4, half(i, 1, 0), 1)
        firsts[i][1].wait_recv()
        add_into(half(i, 3, 1), r1.at[i, 1])
        firsts[i][5] = send_first(i, 5, half(i, 3, 1), 3)

    def turn_corner(i):
        for slot in (2, 3, 4, 5):
            firsts[i][slot].wait_recv()
        add_into(half(i, 0, 0), r1.at[i, 3], r1.at[i, 4])
        add_into(half(i, 0, 1), r1.at[i, 2], r1.at[i, 5])
        seconds[i] = []
        for d in (2, 1, 3):
            copy = pltpu.make_async_remote_copy(
                src_ref=own.at[i, spot, lax.rem(spot_other + d, 4)], dst_ref=r2.at[i, d - 1],
                send_sem=second_sem.at[0, i, d - 1], recv_sem=second_sem.at[1, i, d - 1],
                device_id=second_ring(d), device_id_type=MESH,
            )
            copy.start()
            sent.append(copy)
            seconds[i].append(copy)

    def climb(i):
        for copy in seconds[i]:
            copy.wait_recv()
        up[i] = own[i, spot, spot_other] + r2[i, 0] + r2[i, 1] + r2[i, 2]
        for k in range(2):
            goal = 2 * i + k

            @pl.when(z == goal)
            def _():
                r3[z] = up[i, k]

            @pl.when(z != goal)
            def _():
                pltpu.make_async_remote_copy(
                    src_ref=up.at[i, k], dst_ref=r3.at[z],
                    send_sem=z_sem.at[0], recv_sem=z_sem.at[1],
                    device_id=(dp, goal * NY + y), device_id_type=MESH,
                ).start()

    def out_block(m, i):
        cols = slice(i * 256, (i + 1) * 256)
        mixed = lax.dot_general(
            pairs[1 - m], wio[1 - m, cols, :], (((1,), (1,)), ((), ())), preferred_element_type=F32
        )
        (out_ref, ig_ref)[m][:, cols] = (mixed + skip_ref[:, cols] * xc[m, :, cols].astype(F32)).astype(BF16)

    begin(0)
    out_block(0, 0)
    out_block(0, 1)
    begin(1)
    out_block(0, 2)
    out_block(0, 3)
    begin(2)
    out_block(1, 0)
    relay(0)
    begin(3)
    relay(1)
    out_block(1, 1)
    relay(2)
    out_block(1, 2)
    turn_corner(0)
    relay(3)
    out_block(1, 3)
    turn_corner(1)
    turn_corner(2)
    climb(0)
    turn_corner(3)
    climb(1)
    climb(2)
    climb(3)

    column = pltpu.make_async_remote_copy(
        src_ref=r3.at[pl.ds(0, NZ - 1)], dst_ref=r3.at[pl.ds(0, NZ - 1)],
        send_sem=z_sem.at[0], recv_sem=z_sem.at[1],
        device_id=(dp, lax.rem(z + 1, NZ) * NY + y), device_id_type=MESH,
    )
    column.wait_recv()
    piece = r3[0]
    for k in range(1, NZ):
        piece = piece + r3[k]
    mine = core * NX + x
    fin[mine] = piece * SCALE
    for d in (4, 5, 3, 2, 6, 7, 1):
        pltpu.make_async_remote_copy(
            src_ref=fin.at[mine], dst_ref=fin.at[mine],
            send_sem=fin_sem.at[0], recv_sem=fin_sem.at[1],
            device_id=(lax.rem(dp + d, DP), ctx), device_id_type=MESH,
        ).start()
    row = pltpu.make_async_remote_copy(
        src_ref=fin.at[pl.ds(0, DP - 1)], dst_ref=fin.at[pl.ds(0, DP - 1)],
        send_sem=fin_sem.at[0], recv_sem=fin_sem.at[1],
        device_id=(lax.rem(dp + 1, DP), ctx), device_id_type=MESH,
    )
    column.wait_send()
    for i in range(PARTS):
        swap(i).wait_send()
    for copy in sent:
        copy.wait_send()
    row.wait_recv()
    for q in range(NX):
        gin_ref[:, q * 128 : (q + 1) * 128] = fin[q]
        gout_ref[:, q * 128 : (q + 1) * 128] = fin[NX + q]
    row.wait_send()


def store_kernel(*refs):
    sems = refs[8]
    copies = [pltpu.make_async_copy(refs[k], refs[4 + k], sems.at[k]) for k in range(4)]
    for copy in copies:
        copy.start()
    for copy in copies:
        copy.wait()


def on_device(inputs, step_size, decay_rate, frequency, input_proj, output_proj, skip_gain, cotangent):
    vmem = pl.BlockSpec(memory_space=pltpu.VMEM)
    hbm = pl.BlockSpec(memory_space=pltpu.HBM)
    results = [((ROWS, WIDTH), BF16)] * 2 + [((WIDTH // PEERS, 2 * STATES), F32)] * 2
    held = pl.pallas_call(
        kernel,
        out_shape=tuple(pltpu.VMEM(shape, dtype) for shape, dtype in results),
        in_specs=[hbm] * 8,
        out_specs=(vmem,) * 4,
        scratch_shapes=[
            pltpu.VMEM((1, ROWS), F32),
            pltpu.VMEM((1, STATES), F32),
            pltpu.VMEM((1, STATES), F32),
            pltpu.VMEM((1, WIDTH), F32),
            pltpu.VMEM((2, ROWS, WIDTH), BF16),
            pltpu.VMEM((2, WIDTH, 2 * STATES), BF16),
            pltpu.VMEM((2, WIDTH, ROWS), BF16),
            pltpu.VMEM((SUB * PITCH, 128), F32),
            pltpu.VMEM((4, SUB * PITCH, 128), F32),
            pltpu.VMEM((2, 4, SUB * PITCH, 128), F32),
            pltpu.VMEM((2, ROWS, 2 * STATES), BF16),
            pltpu.VMEM((20, SUB, 128), F32),
            pltpu.VMEM((2, 8, 128), F32),
            pltpu.VMEM((PEERS, 8, 128), F32),
            pltpu.VMEM((PARTS, 4, 4, 2, 32, 128), F32),
            pltpu.VMEM((PARTS, 4, 4, 2, 32, 128), F32),
            pltpu.VMEM((PARTS, 4, 4, 2, 32, 128), F32),
            pltpu.VMEM((PARTS, 6, 2, 2, 32, 128), F32),
            pltpu.VMEM((PARTS, 3, 2, 32, 128), F32),
            pltpu.VMEM((PARTS, 2, 32, 128), F32),
            pltpu.VMEM((NZ, 32, 128), F32),
            pltpu.VMEM((DP, 32, 128), F32),
            pltpu.SemaphoreType.DMA((4,)),
            pltpu.SemaphoreType.DMA((4,)),
            pltpu.SemaphoreType.DMA((2,)),
            pltpu.SemaphoreType.DMA((2, PARTS)),
            pltpu.SemaphoreType.DMA((2, PARTS, 6)),
            pltpu.SemaphoreType.DMA((2, PARTS, 3)),
            pltpu.SemaphoreType.DMA((2,)),
            pltpu.SemaphoreType.DMA((2,)),
        ],
        compiler_params=pltpu.CompilerParams(
            collective_id=0, has_side_effects=True, vmem_limit_bytes=60 * 1024 * 1024
        ),
    )(
        inputs.reshape(ROWS, WIDTH), step_size, decay_rate.reshape(1, STATES), frequency.reshape(1, STATES),
        input_proj, output_proj, skip_gain.reshape(1, WIDTH), cotangent.reshape(ROWS, WIDTH),
    )
    out, ig, gin, gout = pl.pallas_call(
        store_kernel,
        out_shape=tuple(jax.ShapeDtypeStruct(shape, dtype) for shape, dtype in results),
        in_specs=[vmem] * 4,
        out_specs=(hbm,) * 4,
        scratch_shapes=[pltpu.SemaphoreType.DMA((4,))],
    )(*(pltpu.with_memory_space_constraint(part, pltpu.VMEM) for part in held))
    return out.reshape(1, ROWS, WIDTH), ig.reshape(1, ROWS, WIDTH), gin, gout


def solution(mesh):
    in_specs = (
        P("dp", "context", None), P("dp", "context"), P(), P(), P(), P(), P(), P("dp", "context", None),
    )
    out_specs = (
        P("dp", "context", None), P("dp", "context", None), P("context", None), P("context", None),
    )
    return jax.shard_map(on_device, mesh=mesh, in_specs=in_specs, out_specs=out_specs, check_vma=False)
```

```python
import jax
import jax.numpy as jnp
from jax import lax
from jax.experimental import pallas as pl
from jax.experimental.pallas import tpu as pltpu
from jax.sharding import PartitionSpec as P

MESH = pl.DeviceIdType.MESH
F32, BF16 = jnp.float32, jnp.bfloat16
ROWS, WIDTH, STATES = 512, 1024, 256
SUB = 8
LAPS = ROWS // SUB
PITCH = LAPS + 1
NX, NY, NZ = 4, 4, 8
PEERS = NY * NZ
DP = 2 * NX
PARTS = 4
SCALE = float(8 * 16384) ** -0.5


def turn(time, decay, frequency):
    damping = jnp.exp(-(time * decay))
    phase = time * frequency
    n = jnp.floor(phase * 0.6366197723675814 + 0.5)
    r = ((phase - n * 1.5703125) - n * 4.837512969970703125e-4) - n * 7.54978995489188216e-8
    q = n.astype(jnp.int32)
    z = r * r
    sine = r + r * z * (-1.6666654611e-1 + z * (8.3321608736e-3 + z * -1.9515295891e-4))
    cosine = (1.0 - 0.5 * z) + z * z * (
        4.166664568298827e-2 + z * (-1.388731625493765e-3 + z * 2.443315711809948e-5)
    )
    swap = (q & 1) == 1
    a = jnp.where(swap, sine, cosine)
    b = jnp.where(swap, cosine, sine)
    re = jnp.where(((q + 1) & 2) == 2, -a, a)
    im = jnp.where((q & 2) == 2, -b, b)
    return damping * re, damping * im


def cmul(ar, ai, br, bi):
    return ar * br - ai * bi, ar * bi + ai * br


def cmulc(ar, ai, br, bi):
    return ar * br + ai * bi, ar * bi - ai * br


def kernel(
    x_hbm, step_hbm, decay_hbm, freq_hbm, win_hbm, wout_hbm, skip_hbm, cot_hbm,
    out_ref, ig_ref, gin_ref, gout_ref,
    step_ref, decay_ref, freq_ref, skip_ref, xc, wio, xct, stb, lam, drv, pairs, chunk, msg, rmsg, own, theirs, partner,
    r1, r2, up, r3, fin,
    small_sem, load_sem, pre_sem, pair_sem, ring_sem, second_sem, z_sem, fin_sem,
):
    dp = lax.axis_index("dp")
    ctx = lax.axis_index("context")
    core, x = lax.rem(dp, 2), lax.div(dp, 2)
    y, z = lax.rem(ctx, NY), lax.div(ctx, NY)
    other = 1 - core

    barrier = pltpu.get_barrier_semaphore()

    def greet_context(d, _):
        pl.semaphore_signal(barrier, inc=1, device_id=(dp, lax.rem(ctx + d, PEERS)), device_id_type=MESH)
        return 0

    def greet_dp(d, _):
        pl.semaphore_signal(barrier, inc=1, device_id=(lax.rem(dp + d, DP), ctx), device_id_type=MESH)
        return 0

    small = [
        pltpu.make_async_copy(src, dst, small_sem.at[k])
        for k, (src, dst) in enumerate(
            ((step_hbm, step_ref), (decay_hbm, decay_ref), (freq_hbm, freq_ref), (skip_hbm, skip_ref))
        )
    ]
    loads = [
        pltpu.make_async_copy(x_hbm, xc.at[0], load_sem.at[0]),
        pltpu.make_async_copy(win_hbm, wio.at[0], load_sem.at[1]),
        pltpu.make_async_copy(cot_hbm, xc.at[1], load_sem.at[2]),
        pltpu.make_async_copy(wout_hbm, wio.at[1], load_sem.at[3]),
    ]
    for load in small + loads:
        load.start()
    lax.fori_loop(1, PEERS, greet_context, 0)
    lax.fori_loop(1, DP, greet_dp, 0)

    for load in small:
        load.wait()
    decay = [decay_ref[:, g * 128 : (g + 1) * 128] for g in range(2)]
    freq = [freq_ref[:, g * 128 : (g + 1) * 128] for g in range(2)]
    gain = []
    for g in range(2):
        v = 2.0 * decay[g]
        s = jnp.ones_like(v)
        for k in range(9, 1, -1):
            s = 1.0 - v * (1.0 / k) * s
        gain.append(jnp.sqrt(v * s))

    for r in range(ROWS // 128):
        line = jnp.broadcast_to(step_ref[:, r * 128 : (r + 1) * 128], (128, 128))
        turned = line.T
        for s in (0, 1):
            stb[pl.ds((2 * r + s) * PITCH, LAPS), :] = turned[s * LAPS : (s + 1) * LAPS]

    def lam_block(i, _):
        rows = pl.ds(lax.div(i, 2) * PITCH + lax.rem(i, 2) * 32, 32)
        st = stb[rows, :]
        for g in range(2):
            re, im = turn(st, decay[g], freq[g])
            lam[g, rows, :] = re
            lam[2 + g, rows, :] = im
        return 0

    lax.fori_loop(0, ROWS // 32, lam_block, 0)

    for m in range(2):
        loads[2 * m].wait()
        loads[2 * m + 1].wait()
        for nb in range(2):
            res = jnp.dot(xc[m], wio[m, :, nb * 256 : (nb + 1) * 256], preferred_element_type=F32)
            for g in range(2):
                part = res[:, g * 128 : (g + 1) * 128]
                part = part * gain[g] if m == 0 else part
                for s in range(SUB):
                    drv[m, 2 * nb + g, s * PITCH : s * PITCH + LAPS, :] = part[s * LAPS : (s + 1) * LAPS]

    def scan_step(j, carry, store):
        f, b, total = carry[:4], carry[4:8], carry[8]
        rf = pl.ds(j, SUB, stride=PITCH)
        rb = pl.ds(LAPS - 1 - j, SUB, stride=PITCH)
        nf, nb = [None] * 4, [None] * 4
        for g in range(2):
            re, im = cmul(lam[g, rf, :], lam[2 + g, rf, :], f[g], f[2 + g])
            nf[g] = re + drv[0, g, rf, :]
            nf[2 + g] = im + drv[0, 2 + g, rf, :]
            ar = drv[1, g, rb, :] + b[g]
            ai = drv[1, 2 + g, rb, :] + b[2 + g]
            if store:
                drv[0, g, rf, :] = nf[g]
                drv[0, 2 + g, rf, :] = nf[2 + g]
                drv[1, g, rb, :] = ar
                drv[1, 2 + g, rb, :] = ai
            nb[g], nb[2 + g] = cmulc(lam[g, rb, :], lam[2 + g, rb, :], ar, ai)
        if not store:
            total = total + stb[rf, :]
        return (*nf, *nb, total)

    zero = jnp.zeros((SUB, 128), F32)
    summary = lax.fori_loop(0, LAPS, lambda j, c: scan_step(j, c, False), (zero,) * 9, unroll=4)
    for k in range(8):
        chunk[4 + k] = summary[k]
    for g in range(2):
        chunk[g], chunk[2 + g] = turn(jnp.minimum(summary[8], 8.0e6), decay[g], freq[g])
    msg[...] = jnp.zeros_like(msg)

    def pass_chunks():
        f, b = [jnp.zeros((1, 128), F32)] * 4, [jnp.zeros((1, 128), F32)] * 4
        for s in range(SUB):
            e = SUB - 1 - s
            for g in range(2):
                for h in (g, 2 + g):
                    chunk[12 + h, s : s + 1, :] = f[h]
                    chunk[16 + h, e : e + 1, :] = b[h]
                re, im = cmul(chunk[g, s : s + 1, :], chunk[2 + g, s : s + 1, :], f[g], f[2 + g])
                f[g] = re + chunk[4 + g, s : s + 1, :]
                f[2 + g] = im + chunk[6 + g, s : s + 1, :]
                re, im = cmulc(chunk[g, e : e + 1, :], chunk[2 + g, e : e + 1, :], b[g], b[2 + g])
                b[g] = re + chunk[8 + g, e : e + 1, :]
                b[2 + g] = im + chunk[10 + g, e : e + 1, :]
        return f + b

    leave = pass_chunks()
    total = jnp.sum(summary[8], axis=0, keepdims=True)
    for k in range(4):
        msg[0, k : k + 1, :] = leave[k]
        msg[1, k : k + 1, :] = leave[4 + k]
    msg[0, 4:5, :] = total
    msg[1, 4:5, :] = total
    rmsg[ctx] = jnp.zeros((8, 128), F32)

    pl.semaphore_wait(barrier, PEERS - 1 + DP - 1)

    for dz in (4, 3, 5, 2, 6, 1, 7, 0):
        for dy in (2, 1, 3, 0):
            if dz or dy:
                peer = lax.rem(z + dz, NZ) * NY + lax.rem(y + dy, NY)
                pltpu.make_async_remote_copy(
                    src_ref=msg.at[(peer < ctx).astype(jnp.int32), pl.ds(0, 5)], dst_ref=rmsg.at[ctx, pl.ds(0, 5)],
                    send_sem=pre_sem.at[0], recv_sem=pre_sem.at[1],
                    device_id=(dp, peer), device_id_type=MESH,
                ).start()

    line = lax.broadcasted_iota(jnp.int32, (SUB, 128), 0)
    ahead = behind = jnp.zeros((SUB, 128), F32)
    for s in range(SUB):
        ahead = ahead + jnp.where(line > s, summary[8][s : s + 1], 0.0)
        behind = behind + jnp.where(line < s, summary[8][s : s + 1], 0.0)
    for g in range(2):
        chunk[20 + g], chunk[22 + g] = turn(jnp.minimum(ahead, 8.0e6), decay[g], freq[g])
        chunk[24 + g], chunk[26 + g] = turn(jnp.minimum(behind, 8.0e6), decay[g], freq[g])

    for m in range(2):
        def turn_block(i, _, m=m):
            cols = pl.ds(pl.multiple_of(i * 128, 128), 128)
            xct[m, cols, :] = xc[m, :, cols].T
            return 0

        lax.fori_loop(0, WIDTH // 128, turn_block, 0)

    everyone = pltpu.make_async_remote_copy(
        src_ref=rmsg.at[pl.ds(0, PEERS - 1), pl.ds(0, 5)], dst_ref=rmsg.at[pl.ds(0, PEERS - 1), pl.ds(0, 5)],
        send_sem=pre_sem.at[0], recv_sem=pre_sem.at[1],
        device_id=(dp, lax.rem(ctx + 1, PEERS)), device_id_type=MESH,
    )
    everyone.wait_recv()
    everyone.wait_send()

    place = lax.broadcasted_iota(jnp.int32, (PEERS, 128), 0)
    gap = jnp.zeros((PEERS, 128), F32)
    for i in range(PEERS):
        side = 2 * (i < ctx).astype(jnp.int32) - 1
        gap = gap + jnp.where((i - place) * side > 0, rmsg[i, 4:5, :], 0.0)
    gap = jnp.minimum(gap, 8.0e6)
    sign = jnp.where(place < ctx, 1.0, -1.0)
    entering = [None] * 8
    for g in range(2):
        wr, wi = turn(gap, decay[g], sign * freq[g])
        re, im = cmul(wr, wi, rmsg[:, g, :], rmsg[:, 2 + g, :])
        for h, v in ((g, re), (2 + g, im)):
            entering[h] = jnp.sum(jnp.where(place < ctx, v, 0.0), axis=0, keepdims=True)
            entering[4 + h] = jnp.sum(jnp.where(place > ctx, v, 0.0), axis=0, keepdims=True)
    start = [None] * 8
    for g in range(2):
        re, im = cmul(chunk[20 + g], chunk[22 + g], entering[g], entering[2 + g])
        start[g], start[2 + g] = chunk[12 + g] + re, chunk[14 + g] + im
        re, im = cmulc(chunk[24 + g], chunk[26 + g], entering[4 + g], entering[6 + g])
        start[4 + g], start[6 + g] = chunk[16 + g] + re, chunk[18 + g] + im
    start = (*start, zero)
    lax.fori_loop(0, LAPS, lambda j, c: scan_step(j, c, True), start, unroll=4)

    def round_block(i, _):
        rows = pl.ds(pl.multiple_of(i * 32, 32), 32)
        held = pl.ds(lax.div(i, 2) * PITCH + lax.rem(i, 2) * 32, 32)
        for k in range(4):
            pairs[0, rows, k * 128 : (k + 1) * 128] = (drv[1, k, held, :] * gain[k % 2]).astype(BF16)
            pairs[1, rows, k * 128 : (k + 1) * 128] = drv[0, k, held, :].astype(BF16)
        return 0

    lax.fori_loop(0, ROWS // 32, round_block, 0)

    def gradient(m, into, block):
        res = jnp.dot(xct[m, block * 512 : (block + 1) * 512, :], pairs[m], preferred_element_type=F32)
        for zi in range(4):
            for yy in range(NY):
                top = (zi * NY + yy) * 32
                for q in range(NX):
                    a = q + m * (yy - q)
                    b = yy + m * (q - yy)
                    into[2 * block + zi // 2, a, b, zi % 2] = res[top : top + 32, q * 128 : (q + 1) * 128]

    spot = x + core * (y - x)
    spot_other = y + core * (x - y)

    def swap(i):
        return pltpu.make_async_remote_copy(
            src_ref=theirs.at[i], dst_ref=partner.at[i],
            send_sem=pair_sem.at[0, i], recv_sem=pair_sem.at[1, i],
            device_id=(2 * x + other, ctx), device_id_type=MESH,
        )

    for block in range(2):
        gradient(other, theirs, block)
        swap(2 * block).start()
        swap(2 * block + 1).start()
    for block in range(2):
        gradient(core, own, block)

    def first_ring(d):
        return (2 * lax.rem(x + other * d, 4) + core, z * NY + lax.rem(y + core * d, 4))

    def second_ring(d):
        return (2 * lax.rem(x + core * d, 4) + core, z * NY + lax.rem(y + other * d, 4))

    def half(i, d, h):
        return own.at[i, lax.rem(spot + d, 4), pl.ds(2 * h, 2)]

    def add_into(view, *bufs):
        total = view[...]
        for buf in bufs:
            total = total + buf[...]
        view[...] = total

    sent = []

    def send_first(i, slot, src, d):
        copy = pltpu.make_async_remote_copy(
            src_ref=src, dst_ref=r1.at[i, slot], send_sem=ring_sem.at[0, i, slot], recv_sem=ring_sem.at[1, i, slot],
            device_id=first_ring(d), device_id_type=MESH,
        )
        copy.start()
        sent.append(copy)
        return copy

    firsts = [[None] * 6 for _ in range(PARTS)]
    seconds = [None] * PARTS

    def begin(i):
        swap(i).wait_recv()

        def add(a, _):
            own[i, a] += partner[i, a]
            return 0

        lax.fori_loop(0, 4, add, 0)
        firsts[i][0] = send_first(i, 0, half(i, 2, 0), 1)
        firsts[i][1] = send_first(i, 1, half(i, 2, 1), 3)
        firsts[i][2] = send_first(i, 2, half(i, 1, 1), 1)
        firsts[i][3] = send_first(i, 3, half(i, 3, 0), 3)

    def relay(i):
        firsts[i][0].wait_recv()
        add_into(half(i, 1, 0), r1.at[i, 0])
        firsts[i][4] = send_first(i, 4, half(i, 1, 0), 1)
        firsts[i][1].wait_recv()
        add_into(half(i, 3, 1), r1.at[i, 1])
        firsts[i][5] = send_first(i, 5, half(i, 3, 1), 3)

    def turn_corner(i):
        for slot in (2, 3, 4, 5):
            firsts[i][slot].wait_recv()
        add_into(half(i, 0, 0), r1.at[i, 3], r1.at[i, 4])
        add_into(half(i, 0, 1), r1.at[i, 2], r1.at[i, 5])
        seconds[i] = []
        for d in (2, 1, 3):
            copy = pltpu.make_async_remote_copy(
                src_ref=own.at[i, spot, lax.rem(spot_other + d, 4)], dst_ref=r2.at[i, d - 1],
                send_sem=second_sem.at[0, i, d - 1], recv_sem=second_sem.at[1, i, d - 1],
                device_id=second_ring(d), device_id_type=MESH,
            )
            copy.start()
            sent.append(copy)
            seconds[i].append(copy)

    def climb(i):
        for copy in seconds[i]:
            copy.wait_recv()
        up[i] = own[i, spot, spot_other] + r2[i, 0] + r2[i, 1] + r2[i, 2]
        for k in range(2):
            goal = 2 * i + k

            @pl.when(z == goal)
            def _():
                r3[z] = up[i, k]

            @pl.when(z != goal)
            def _():
                pltpu.make_async_remote_copy(
                    src_ref=up.at[i, k], dst_ref=r3.at[z],
                    send_sem=z_sem.at[0], recv_sem=z_sem.at[1],
                    device_id=(dp, goal * NY + y), device_id_type=MESH,
                ).start()

    def out_block(m, i):
        cols = slice(i * 256, (i + 1) * 256)
        mixed = lax.dot_general(
            pairs[1 - m], wio[1 - m, cols, :], (((1,), (1,)), ((), ())), preferred_element_type=F32
        )
        (out_ref, ig_ref)[m][:, cols] = (mixed + skip_ref[:, cols] * xc[m, :, cols].astype(F32)).astype(BF16)

    begin(0)
    out_block(0, 0)
    out_block(0, 1)
    begin(1)
    out_block(0, 2)
    out_block(0, 3)
    begin(2)
    out_block(1, 0)
    relay(0)
    begin(3)
    relay(1)
    out_block(1, 1)
    relay(2)
    out_block(1, 2)
    turn_corner(0)
    relay(3)
    out_block(1, 3)
    turn_corner(1)
    turn_corner(2)
    climb(0)
    turn_corner(3)
    climb(1)
    climb(2)
    climb(3)

    column = pltpu.make_async_remote_copy(
        src_ref=r3.at[pl.ds(0, NZ - 1)], dst_ref=r3.at[pl.ds(0, NZ - 1)],
        send_sem=z_sem.at[0], recv_sem=z_sem.at[1],
        device_id=(dp, lax.rem(z + 1, NZ) * NY + y), device_id_type=MESH,
    )
    column.wait_recv()
    piece = r3[0]
    for k in range(1, NZ):
        piece = piece + r3[k]
    mine = core * NX + x
    fin[mine] = piece * SCALE
    for d in (4, 5, 3, 2, 6, 7, 1):
        pltpu.make_async_remote_copy(
            src_ref=fin.at[mine], dst_ref=fin.at[mine],
            send_sem=fin_sem.at[0], recv_sem=fin_sem.at[1],
            device_id=(lax.rem(dp + d, DP), ctx), device_id_type=MESH,
        ).start()
    row = pltpu.make_async_remote_copy(
        src_ref=fin.at[pl.ds(0, DP - 1)], dst_ref=fin.at[pl.ds(0, DP - 1)],
        send_sem=fin_sem.at[0], recv_sem=fin_sem.at[1],
        device_id=(lax.rem(dp + 1, DP), ctx), device_id_type=MESH,
    )
    column.wait_send()
    for i in range(PARTS):
        swap(i).wait_send()
    for copy in sent:
        copy.wait_send()
    row.wait_recv()
    for q in range(NX):
        gin_ref[:, q * 128 : (q + 1) * 128] = fin[q]
        gout_ref[:, q * 128 : (q + 1) * 128] = fin[NX + q]
    row.wait_send()


def store_kernel(*refs):
    sems = refs[8]
    copies = [pltpu.make_async_copy(refs[k], refs[4 + k], sems.at[k]) for k in range(4)]
    for copy in copies:
        copy.start()
    for copy in copies:
        copy.wait()


def on_device(inputs, step_size, decay_rate, frequency, input_proj, output_proj, skip_gain, cotangent):
    vmem = pl.BlockSpec(memory_space=pltpu.VMEM)
    hbm = pl.BlockSpec(memory_space=pltpu.HBM)
    results = [((ROWS, WIDTH), BF16)] * 2 + [((WIDTH // PEERS, 2 * STATES), F32)] * 2
    held = pl.pallas_call(
        kernel,
        out_shape=tuple(pltpu.VMEM(shape, dtype) for shape, dtype in results),
        in_specs=[hbm] * 8,
        out_specs=(vmem,) * 4,
        scratch_shapes=[
            pltpu.VMEM((1, ROWS), F32),
            pltpu.VMEM((1, STATES), F32),
            pltpu.VMEM((1, STATES), F32),
            pltpu.VMEM((1, WIDTH), F32),
            pltpu.VMEM((2, ROWS, WIDTH), BF16),
            pltpu.VMEM((2, WIDTH, 2 * STATES), BF16),
            pltpu.VMEM((2, WIDTH, ROWS), BF16),
            pltpu.VMEM((SUB * PITCH, 128), F32),
            pltpu.VMEM((4, SUB * PITCH, 128), F32),
            pltpu.VMEM((2, 4, SUB * PITCH, 128), F32),
            pltpu.VMEM((2, ROWS, 2 * STATES), BF16),
            pltpu.VMEM((28, SUB, 128), F32),
            pltpu.VMEM((2, 8, 128), F32),
            pltpu.VMEM((PEERS, 8, 128), F32),
            pltpu.VMEM((PARTS, 4, 4, 2, 32, 128), F32),
            pltpu.VMEM((PARTS, 4, 4, 2, 32, 128), F32),
            pltpu.VMEM((PARTS, 4, 4, 2, 32, 128), F32),
            pltpu.VMEM((PARTS, 6, 2, 2, 32, 128), F32),
            pltpu.VMEM((PARTS, 3, 2, 32, 128), F32),
            pltpu.VMEM((PARTS, 2, 32, 128), F32),
            pltpu.VMEM((NZ, 32, 128), F32),
            pltpu.VMEM((DP, 32, 128), F32),
            pltpu.SemaphoreType.DMA((4,)),
            pltpu.SemaphoreType.DMA((4,)),
            pltpu.SemaphoreType.DMA((2,)),
            pltpu.SemaphoreType.DMA((2, PARTS)),
            pltpu.SemaphoreType.DMA((2, PARTS, 6)),
            pltpu.SemaphoreType.DMA((2, PARTS, 3)),
            pltpu.SemaphoreType.DMA((2,)),
            pltpu.SemaphoreType.DMA((2,)),
        ],
        compiler_params=pltpu.CompilerParams(
            collective_id=0, has_side_effects=True, vmem_limit_bytes=60 * 1024 * 1024
        ),
    )(
        inputs.reshape(ROWS, WIDTH), step_size, decay_rate.reshape(1, STATES), frequency.reshape(1, STATES),
        input_proj, output_proj, skip_gain.reshape(1, WIDTH), cotangent.reshape(ROWS, WIDTH),
    )
    out, ig, gin, gout = pl.pallas_call(
        store_kernel,
        out_shape=tuple(jax.ShapeDtypeStruct(shape, dtype) for shape, dtype in results),
        in_specs=[vmem] * 4,
        out_specs=(hbm,) * 4,
        scratch_shapes=[pltpu.SemaphoreType.DMA((4,))],
    )(*(pltpu.with_memory_space_constraint(part, pltpu.VMEM) for part in held))
    return out.reshape(1, ROWS, WIDTH), ig.reshape(1, ROWS, WIDTH), gin, gout


def solution(mesh):
    in_specs = (
        P("dp", "context", None), P("dp", "context"), P(), P(), P(), P(), P(), P("dp", "context", None),
    )
    out_specs = (
        P("dp", "context", None), P("dp", "context", None), P("context", None), P("context", None),
    )
    return jax.shard_map(on_device, mesh=mesh, in_specs=in_specs, out_specs=out_specs, check_vma=False)
```

```python
import jax
import jax.numpy as jnp
from jax import lax
from jax.experimental import pallas as pl
from jax.experimental.pallas import tpu as pltpu
from jax.sharding import PartitionSpec as P

MESH = pl.DeviceIdType.MESH
F32, BF16 = jnp.float32, jnp.bfloat16
ROWS, WIDTH, STATES = 512, 1024, 256
SUB = 8
LAPS = ROWS // SUB
PITCH = LAPS + 1
NX, NY, NZ = 4, 4, 8
PEERS = NY * NZ
DP = 2 * NX
PARTS = 4
SCALE = float(8 * 16384) ** -0.5


def turn(time, decay, frequency):
    damping = jnp.exp(-(time * decay))
    phase = time * frequency
    n = jnp.floor(phase * 0.6366197723675814 + 0.5)
    r = ((phase - n * 1.5703125) - n * 4.837512969970703125e-4) - n * 7.54978995489188216e-8
    q = n.astype(jnp.int32)
    z = r * r
    sine = r + r * z * (-1.6666654611e-1 + z * (8.3321608736e-3 + z * -1.9515295891e-4))
    cosine = (1.0 - 0.5 * z) + z * z * (
        4.166664568298827e-2 + z * (-1.388731625493765e-3 + z * 2.443315711809948e-5)
    )
    swap = (q & 1) == 1
    a = jnp.where(swap, sine, cosine)
    b = jnp.where(swap, cosine, sine)
    re = jnp.where(((q + 1) & 2) == 2, -a, a)
    im = jnp.where((q & 2) == 2, -b, b)
    return damping * re, damping * im


def cmul(ar, ai, br, bi):
    return ar * br - ai * bi, ar * bi + ai * br


def cmulc(ar, ai, br, bi):
    return ar * br + ai * bi, ar * bi - ai * br


def kernel(
    x_hbm, step_hbm, decay_hbm, freq_hbm, win_hbm, wout_hbm, skip_hbm, cot_hbm,
    out_ref, ig_ref, gin_ref, gout_ref,
    step_ref, decay_ref, freq_ref, skip_ref, xc, wio, xct, stb, lam, drv, pairs, chunk, msg, rmsg, own, theirs, partner,
    r1, r2, up, r3, fin,
    small_sem, load_sem, pre_sem, quarter_sem, pair_sem, ring_sem, second_sem, z_sem, fin_sem,
):
    dp = lax.axis_index("dp")
    ctx = lax.axis_index("context")
    core, x = lax.rem(dp, 2), lax.div(dp, 2)
    y, z = lax.rem(ctx, NY), lax.div(ctx, NY)
    other = 1 - core

    barrier = pltpu.get_barrier_semaphore()

    def greet_context(d, _):
        pl.semaphore_signal(barrier, inc=1, device_id=(dp, lax.rem(ctx + d, PEERS)), device_id_type=MESH)
        return 0

    def greet_dp(d, _):
        pl.semaphore_signal(barrier, inc=1, device_id=(lax.rem(dp + d, DP), ctx), device_id_type=MESH)
        return 0

    small = [
        pltpu.make_async_copy(src, dst, small_sem.at[k])
        for k, (src, dst) in enumerate(
            ((step_hbm, step_ref), (decay_hbm, decay_ref), (freq_hbm, freq_ref), (skip_hbm, skip_ref))
        )
    ]
    loads = [
        pltpu.make_async_copy(x_hbm, xc.at[0], load_sem.at[0]),
        pltpu.make_async_copy(win_hbm, wio.at[0], load_sem.at[1]),
        pltpu.make_async_copy(cot_hbm, xc.at[1], load_sem.at[2]),
        pltpu.make_async_copy(wout_hbm, wio.at[1], load_sem.at[3]),
    ]
    for load in small + loads:
        load.start()
    lax.fori_loop(1, PEERS, greet_context, 0)
    lax.fori_loop(1, DP, greet_dp, 0)

    for load in small:
        load.wait()
    decay = [decay_ref[:, g * 128 : (g + 1) * 128] for g in range(2)]
    freq = [freq_ref[:, g * 128 : (g + 1) * 128] for g in range(2)]
    gain = []
    for g in range(2):
        v = 2.0 * decay[g]
        s = jnp.ones_like(v)
        for k in range(9, 1, -1):
            s = 1.0 - v * (1.0 / k) * s
        gain.append(jnp.sqrt(v * s))

    for r in range(ROWS // 128):
        line = jnp.broadcast_to(step_ref[:, r * 128 : (r + 1) * 128], (128, 128))
        turned = line.T
        for s in (0, 1):
            stb[pl.ds((2 * r + s) * PITCH, LAPS), :] = turned[s * LAPS : (s + 1) * LAPS]

    def lam_block(i):
        rows = pl.ds((i // 2) * PITCH + (i % 2) * 32, 32)
        st = stb[rows, :]
        for g in range(2):
            re, im = turn(st, decay[g], freq[g])
            lam[g, rows, :] = re
            lam[2 + g, rows, :] = im

    for m in range(2):
        loads[2 * m].wait()
        loads[2 * m + 1].wait()
        for nb in range(2):
            res = jnp.dot(xc[m], wio[m, :, nb * 256 : (nb + 1) * 256], preferred_element_type=F32)
            for g in range(2):
                part = res[:, g * 128 : (g + 1) * 128]
                part = part * gain[g] if m == 0 else part
                for s in range(SUB):
                    drv[m, 2 * nb + g, s * PITCH : s * PITCH + LAPS, :] = part[s * LAPS : (s + 1) * LAPS]
            for i in range(4):
                lam_block(8 * m + 4 * nb + i)

    def scan_step(j, carry, store):
        f, b, total = carry[:4], carry[4:8], carry[8]
        rf = pl.ds(j, SUB, stride=PITCH)
        rb = pl.ds(LAPS - 1 - j, SUB, stride=PITCH)
        nf, nb = [None] * 4, [None] * 4
        for g in range(2):
            re, im = cmul(lam[g, rf, :], lam[2 + g, rf, :], f[g], f[2 + g])
            nf[g] = re + drv[0, g, rf, :]
            nf[2 + g] = im + drv[0, 2 + g, rf, :]
            ar = drv[1, g, rb, :] + b[g]
            ai = drv[1, 2 + g, rb, :] + b[2 + g]
            if store:
                drv[0, g, rf, :] = nf[g]
                drv[0, 2 + g, rf, :] = nf[2 + g]
                drv[1, g, rb, :] = ar
                drv[1, 2 + g, rb, :] = ai
            nb[g], nb[2 + g] = cmulc(lam[g, rb, :], lam[2 + g, rb, :], ar, ai)
        if not store:
            total = total + stb[rf, :]
        return (*nf, *nb, total)

    zero = jnp.zeros((SUB, 128), F32)
    summary = lax.fori_loop(0, LAPS, lambda j, c: scan_step(j, c, False), (zero,) * 9, unroll=4)
    for k in range(8):
        chunk[4 + k] = summary[k]
    for g in range(2):
        chunk[g], chunk[2 + g] = turn(jnp.minimum(summary[8], 8.0e6), decay[g], freq[g])
    msg[...] = jnp.zeros_like(msg)

    def pass_chunks():
        f, b = [jnp.zeros((1, 128), F32)] * 4, [jnp.zeros((1, 128), F32)] * 4
        for s in range(SUB):
            e = SUB - 1 - s
            for g in range(2):
                for h in (g, 2 + g):
                    chunk[12 + h, s : s + 1, :] = f[h]
                    chunk[16 + h, e : e + 1, :] = b[h]
                re, im = cmul(chunk[g, s : s + 1, :], chunk[2 + g, s : s + 1, :], f[g], f[2 + g])
                f[g] = re + chunk[4 + g, s : s + 1, :]
                f[2 + g] = im + chunk[6 + g, s : s + 1, :]
                re, im = cmulc(chunk[g, e : e + 1, :], chunk[2 + g, e : e + 1, :], b[g], b[2 + g])
                b[g] = re + chunk[8 + g, e : e + 1, :]
                b[2 + g] = im + chunk[10 + g, e : e + 1, :]
        return f + b

    leave = pass_chunks()
    total = jnp.sum(summary[8], axis=0, keepdims=True)
    for k in range(4):
        msg[0, k : k + 1, :] = leave[k]
        msg[1, k : k + 1, :] = leave[4 + k]
    msg[0, 4:5, :] = total
    msg[1, 4:5, :] = total
    rmsg[ctx] = jnp.zeros((8, 128), F32)

    pl.semaphore_wait(barrier, PEERS - 1 + DP - 1)

    for dz in (4, 3, 5, 2, 6, 1, 7, 0):
        for dy in (2, 1, 3, 0):
            if dz or dy:
                peer = lax.rem(z + dz, NZ) * NY + lax.rem(y + dy, NY)
                pltpu.make_async_remote_copy(
                    src_ref=msg.at[(peer < ctx).astype(jnp.int32), pl.ds(0, 5)], dst_ref=rmsg.at[ctx, pl.ds(0, 5)],
                    send_sem=pre_sem.at[0], recv_sem=pre_sem.at[1],
                    device_id=(dp, peer), device_id_type=MESH,
                ).start()

    line = lax.broadcasted_iota(jnp.int32, (SUB, 128), 0)
    ahead = behind = jnp.zeros((SUB, 128), F32)
    for s in range(SUB):
        ahead = ahead + jnp.where(line > s, summary[8][s : s + 1], 0.0)
        behind = behind + jnp.where(line < s, summary[8][s : s + 1], 0.0)
    for g in range(2):
        chunk[20 + g], chunk[22 + g] = turn(jnp.minimum(ahead, 8.0e6), decay[g], freq[g])
        chunk[24 + g], chunk[26 + g] = turn(jnp.minimum(behind, 8.0e6), decay[g], freq[g])

    for m in range(2):
        def turn_block(i, _, m=m):
            cols = pl.ds(pl.multiple_of(i * 128, 128), 128)
            xct[m, cols, :] = xc[m, :, cols].T
            return 0

        lax.fori_loop(0, WIDTH // 128, turn_block, 0)

    everyone = pltpu.make_async_remote_copy(
        src_ref=rmsg.at[pl.ds(0, PEERS - 1), pl.ds(0, 5)], dst_ref=rmsg.at[pl.ds(0, PEERS - 1), pl.ds(0, 5)],
        send_sem=pre_sem.at[0], recv_sem=pre_sem.at[1],
        device_id=(dp, lax.rem(ctx + 1, PEERS)), device_id_type=MESH,
    )
    everyone.wait_recv()
    everyone.wait_send()

    place = lax.broadcasted_iota(jnp.int32, (PEERS, 128), 0)
    gap = jnp.zeros((PEERS, 128), F32)
    for i in range(PEERS):
        side = 2 * (i < ctx).astype(jnp.int32) - 1
        gap = gap + jnp.where((i - place) * side > 0, rmsg[i, 4:5, :], 0.0)
    gap = jnp.minimum(gap, 8.0e6)
    sign = jnp.where(place < ctx, 1.0, -1.0)
    entering = [None] * 8
    for g in range(2):
        wr, wi = turn(gap, decay[g], sign * freq[g])
        re, im = cmul(wr, wi, rmsg[:, g, :], rmsg[:, 2 + g, :])
        for h, v in ((g, re), (2 + g, im)):
            entering[h] = jnp.sum(jnp.where(place < ctx, v, 0.0), axis=0, keepdims=True)
            entering[4 + h] = jnp.sum(jnp.where(place > ctx, v, 0.0), axis=0, keepdims=True)
    start = [None] * 8
    for g in range(2):
        re, im = cmul(chunk[20 + g], chunk[22 + g], entering[g], entering[2 + g])
        start[g], start[2 + g] = chunk[12 + g] + re, chunk[14 + g] + im
        re, im = cmulc(chunk[24 + g], chunk[26 + g], entering[4 + g], entering[6 + g])
        start[4 + g], start[6 + g] = chunk[16 + g] + re, chunk[18 + g] + im
    start = (*start, zero)
    lax.fori_loop(0, LAPS, lambda j, c: scan_step(j, c, True), start, unroll=4)

    def round_pairs(w):
        scale = [jnp.where(w == 0, gain[g], 1.0) for g in range(2)]

        def round_block(i, _):
            rows = pl.ds(pl.multiple_of(i * 64, 64), 64)
            held = pl.ds(i * PITCH, 64)
            for k in range(4):
                pairs[w, rows, k * 128 : (k + 1) * 128] = (drv[1 - w, k, held, :] * scale[k % 2]).astype(BF16)
            return 0

        lax.fori_loop(0, SUB, round_block, 0)

    def gradient(m, into, block):
        res = jnp.dot(xct[m, block * 512 : (block + 1) * 512, :], pairs[m], preferred_element_type=F32)
        for zi in range(4):
            for yy in range(NY):
                top = (zi * NY + yy) * 32
                for q in range(NX):
                    a = q + m * (yy - q)
                    b = yy + m * (q - yy)
                    into[2 * block + zi // 2, a, b, zi % 2] = res[top : top + 32, q * 128 : (q + 1) * 128]

    spot = x + core * (y - x)
    spot_other = y + core * (x - y)

    def swap(i):
        return pltpu.make_async_remote_copy(
            src_ref=theirs.at[i], dst_ref=partner.at[i],
            send_sem=pair_sem.at[0, i], recv_sem=pair_sem.at[1, i],
            device_id=(2 * x + other, ctx), device_id_type=MESH,
        )

    def swap_quarter(k, theirs_place=None):
        place = spot_other if theirs_place is None else theirs_place
        a = lax.rem(place + (2, 1, 3, 0)[k], 4)
        return pltpu.make_async_remote_copy(
            src_ref=theirs.at[0, a], dst_ref=partner.at[0, a],
            send_sem=quarter_sem.at[0, k], recv_sem=quarter_sem.at[1, k],
            device_id=(2 * x + other, ctx), device_id_type=MESH,
        )

    round_pairs(other)
    gradient(other, theirs, 0)
    for k in range(4):
        swap_quarter(k).start()
    swap(1).start()
    gradient(other, theirs, 1)
    swap(2).start()
    swap(3).start()
    round_pairs(core)
    for block in range(2):
        gradient(core, own, block)

    def first_ring(d):
        return (2 * lax.rem(x + other * d, 4) + core, z * NY + lax.rem(y + core * d, 4))

    def second_ring(d):
        return (2 * lax.rem(x + core * d, 4) + core, z * NY + lax.rem(y + other * d, 4))

    def half(i, d, h):
        return own.at[i, lax.rem(spot + d, 4), pl.ds(2 * h, 2)]

    def add_into(view, *bufs):
        total = view[...]
        for buf in bufs:
            total = total + buf[...]
        view[...] = total

    sent = []

    def send_first(i, slot, src, d):
        copy = pltpu.make_async_remote_copy(
            src_ref=src, dst_ref=r1.at[i, slot], send_sem=ring_sem.at[0, i, slot], recv_sem=ring_sem.at[1, i, slot],
            device_id=first_ring(d), device_id_type=MESH,
        )
        copy.start()
        sent.append(copy)
        return copy

    firsts = [[None] * 6 for _ in range(PARTS)]
    seconds = [None] * PARTS

    def begin(i):
        if i > 0:
            swap(i).wait_recv()
        for k, d in enumerate((2, 1, 3, 0)):
            if i == 0:
                swap_quarter(k, spot).wait_recv()
            a = lax.rem(spot + d, 4)
            own[i, a] += partner[i, a]
            if k == 0:
                firsts[i][0] = send_first(i, 0, half(i, 2, 0), 1)
                firsts[i][1] = send_first(i, 1, half(i, 2, 1), 3)
            elif k == 1:
                firsts[i][2] = send_first(i, 2, half(i, 1, 1), 1)
            elif k == 2:
                firsts[i][3] = send_first(i, 3, half(i, 3, 0), 3)

    def relay(i):
        firsts[i][0].wait_recv()
        add_into(half(i, 1, 0), r1.at[i, 0])
        firsts[i][4] = send_first(i, 4, half(i, 1, 0), 1)
        firsts[i][1].wait_recv()
        add_into(half(i, 3, 1), r1.at[i, 1])
        firsts[i][5] = send_first(i, 5, half(i, 3, 1), 3)

    def turn_corner(i):
        for slot in (2, 3, 4, 5):
            firsts[i][slot].wait_recv()
        add_into(half(i, 0, 0), r1.at[i, 3], r1.at[i, 4])
        add_into(half(i, 0, 1), r1.at[i, 2], r1.at[i, 5])
        seconds[i] = []
        for d in (2, 1, 3):
            copy = pltpu.make_async_remote_copy(
                src_ref=own.at[i, spot, lax.rem(spot_other + d, 4)], dst_ref=r2.at[i, d - 1],
                send_sem=second_sem.at[0, i, d - 1], recv_sem=second_sem.at[1, i, d - 1],
                device_id=second_ring(d), device_id_type=MESH,
            )
            copy.start()
            sent.append(copy)
            seconds[i].append(copy)

    def climb(i):
        for copy in seconds[i]:
            copy.wait_recv()
        up[i] = own[i, spot, spot_other] + r2[i, 0] + r2[i, 1] + r2[i, 2]
        for k in range(2):
            goal = 2 * i + k

            @pl.when(z == goal)
            def _():
                r3[z] = up[i, k]

            @pl.when(z != goal)
            def _():
                pltpu.make_async_remote_copy(
                    src_ref=up.at[i, k], dst_ref=r3.at[z],
                    send_sem=z_sem.at[0], recv_sem=z_sem.at[1],
                    device_id=(dp, goal * NY + y), device_id_type=MESH,
                ).start()

    def out_block(m, i):
        cols = slice(i * 256, (i + 1) * 256)
        mixed = lax.dot_general(
            pairs[1 - m], wio[1 - m, cols, :], (((1,), (1,)), ((), ())), preferred_element_type=F32
        )
        (out_ref, ig_ref)[m][:, cols] = (mixed + skip_ref[:, cols] * xc[m, :, cols].astype(F32)).astype(BF16)

    begin(0)
    out_block(0, 0)
    out_block(0, 1)
    begin(1)
    out_block(0, 2)
    out_block(0, 3)
    begin(2)
    out_block(1, 0)
    relay(0)
    begin(3)
    relay(1)
    out_block(1, 1)
    relay(2)
    out_block(1, 2)
    turn_corner(0)
    relay(3)
    out_block(1, 3)
    turn_corner(1)
    turn_corner(2)
    climb(0)
    turn_corner(3)
    climb(1)
    climb(2)
    climb(3)

    column = pltpu.make_async_remote_copy(
        src_ref=r3.at[pl.ds(0, NZ - 1)], dst_ref=r3.at[pl.ds(0, NZ - 1)],
        send_sem=z_sem.at[0], recv_sem=z_sem.at[1],
        device_id=(dp, lax.rem(z + 1, NZ) * NY + y), device_id_type=MESH,
    )
    column.wait_recv()
    piece = r3[0]
    for k in range(1, NZ):
        piece = piece + r3[k]
    mine = core * NX + x
    fin[mine] = piece * SCALE
    for d in (4, 5, 3, 2, 6, 7, 1):
        pltpu.make_async_remote_copy(
            src_ref=fin.at[mine], dst_ref=fin.at[mine],
            send_sem=fin_sem.at[0], recv_sem=fin_sem.at[1],
            device_id=(lax.rem(dp + d, DP), ctx), device_id_type=MESH,
        ).start()
    row = pltpu.make_async_remote_copy(
        src_ref=fin.at[pl.ds(0, DP - 1)], dst_ref=fin.at[pl.ds(0, DP - 1)],
        send_sem=fin_sem.at[0], recv_sem=fin_sem.at[1],
        device_id=(lax.rem(dp + 1, DP), ctx), device_id_type=MESH,
    )
    column.wait_send()
    for k in range(4):
        swap_quarter(k).wait_send()
    for i in range(1, PARTS):
        swap(i).wait_send()
    for copy in sent:
        copy.wait_send()
    row.wait_recv()
    for q in range(NX):
        gin_ref[:, q * 128 : (q + 1) * 128] = fin[q]
        gout_ref[:, q * 128 : (q + 1) * 128] = fin[NX + q]
    row.wait_send()


def store_kernel(*refs):
    sems = refs[8]
    copies = [pltpu.make_async_copy(refs[k], refs[4 + k], sems.at[k]) for k in range(4)]
    for copy in copies:
        copy.start()
    for copy in copies:
        copy.wait()


def on_device(inputs, step_size, decay_rate, frequency, input_proj, output_proj, skip_gain, cotangent):
    vmem = pl.BlockSpec(memory_space=pltpu.VMEM)
    hbm = pl.BlockSpec(memory_space=pltpu.HBM)
    results = [((ROWS, WIDTH), BF16)] * 2 + [((WIDTH // PEERS, 2 * STATES), F32)] * 2
    held = pl.pallas_call(
        kernel,
        out_shape=tuple(pltpu.VMEM(shape, dtype) for shape, dtype in results),
        in_specs=[hbm] * 8,
        out_specs=(vmem,) * 4,
        scratch_shapes=[
            pltpu.VMEM((1, ROWS), F32),
            pltpu.VMEM((1, STATES), F32),
            pltpu.VMEM((1, STATES), F32),
            pltpu.VMEM((1, WIDTH), F32),
            pltpu.VMEM((2, ROWS, WIDTH), BF16),
            pltpu.VMEM((2, WIDTH, 2 * STATES), BF16),
            pltpu.VMEM((2, WIDTH, ROWS), BF16),
            pltpu.VMEM((SUB * PITCH, 128), F32),
            pltpu.VMEM((4, SUB * PITCH, 128), F32),
            pltpu.VMEM((2, 4, SUB * PITCH, 128), F32),
            pltpu.VMEM((2, ROWS, 2 * STATES), BF16),
            pltpu.VMEM((28, SUB, 128), F32),
            pltpu.VMEM((2, 8, 128), F32),
            pltpu.VMEM((PEERS, 8, 128), F32),
            pltpu.VMEM((PARTS, 4, 4, 2, 32, 128), F32),
            pltpu.VMEM((PARTS, 4, 4, 2, 32, 128), F32),
            pltpu.VMEM((PARTS, 4, 4, 2, 32, 128), F32),
            pltpu.VMEM((PARTS, 6, 2, 2, 32, 128), F32),
            pltpu.VMEM((PARTS, 3, 2, 32, 128), F32),
            pltpu.VMEM((PARTS, 2, 32, 128), F32),
            pltpu.VMEM((NZ, 32, 128), F32),
            pltpu.VMEM((DP, 32, 128), F32),
            pltpu.SemaphoreType.DMA((4,)),
            pltpu.SemaphoreType.DMA((4,)),
            pltpu.SemaphoreType.DMA((2,)),
            pltpu.SemaphoreType.DMA((2, 4)),
            pltpu.SemaphoreType.DMA((2, PARTS)),
            pltpu.SemaphoreType.DMA((2, PARTS, 6)),
            pltpu.SemaphoreType.DMA((2, PARTS, 3)),
            pltpu.SemaphoreType.DMA((2,)),
            pltpu.SemaphoreType.DMA((2,)),
        ],
        compiler_params=pltpu.CompilerParams(
            collective_id=0, has_side_effects=True, vmem_limit_bytes=60 * 1024 * 1024
        ),
    )(
        inputs.reshape(ROWS, WIDTH), step_size, decay_rate.reshape(1, STATES), frequency.reshape(1, STATES),
        input_proj, output_proj, skip_gain.reshape(1, WIDTH), cotangent.reshape(ROWS, WIDTH),
    )
    out, ig, gin, gout = pl.pallas_call(
        store_kernel,
        out_shape=tuple(jax.ShapeDtypeStruct(shape, dtype) for shape, dtype in results),
        in_specs=[vmem] * 4,
        out_specs=(hbm,) * 4,
        scratch_shapes=[pltpu.SemaphoreType.DMA((4,))],
    )(*(pltpu.with_memory_space_constraint(part, pltpu.VMEM) for part in held))
    return out.reshape(1, ROWS, WIDTH), ig.reshape(1, ROWS, WIDTH), gin, gout


def solution(mesh):
    in_specs = (
        P("dp", "context", None), P("dp", "context"), P(), P(), P(), P(), P(), P("dp", "context", None),
    )
    out_specs = (
        P("dp", "context", None), P("dp", "context", None), P("context", None), P("context", None),
    )
    return jax.shard_map(on_device, mesh=mesh, in_specs=in_specs, out_specs=out_specs, check_vma=False)
```
